32 devices in a mesh: grp: 1, storm: 16 (over z, y, x), tile: 2 (over core).
Axes of the slice: x: 2, y: 2, z: 4, core: 2. Of those that a mesh axis runs over, the one named last changes fastest.
Arguments:
- patches: float32 [64, 2, 256, 256], P(('grp', 'storm', 'tile')), may hold values from -4 to 4
- patch_coeffs: float32 [64, 2], P(('grp', 'storm', 'tile')), may hold values from 0.01 to 0.15
- row_offset: int32 [64], P(('grp', 'storm', 'tile')), may hold values from 0 to 768, as said below
- col_offset: int32 [64], P(('grp', 'storm', 'tile')), may hold values from 0 to 1792
- live_counts: int32 [32], P(('grp', 'storm', 'tile')), may hold values from 0 to 2, as said below
- class_map: int32 [1024, 2048], P(('grp', 'storm'), 'tile'), may hold values from 0 to 15
- roughness: float32 [16], replicated, may hold values from 0.2 to 0.9
Outputs:
- smoothed_map: float32 [1024, 2048], P(('grp', 'storm'), 'tile')
The draws below stay inside these ranges and needn't reach their ends.
Inputs may be any that keep to these rules, and one draw needn't show every extreme that they name: `live_counts`: A device's live patches are its first slots. The counts of the two devices whose storm indices differ by half the storm axis, at the same tile index, add up to 2. `row_offset`: each device's first half of its 2 slots lie wholly in the upper half of the map's 1024 rows and its other slots wholly in the lower half; the squares of one device's slots of one half all cover a common map row. So no aligned block of 64 map rows is covered by more than half of one device's slots, and some block is covered by exactly half of them on every device.
All inputs are finite; a program needn't handle non-finite values.
Results may differ from the reference program's by a relative error of at most 0.001.
The reference program's roundings to bfloat16 on the way count: a program that leaves them out, or rounds other values in their place, can miss the bound.
Values may be sent and summed in bfloat16 or wider, within the bound.
No kernel may reach another device: no remote copies, remote signals or barrier semaphores. Data moves between devices by JAX's collectives and lax.ppermute only.
A program may use at most 64 MiB of HBM per device.

```python
import math
import jax
import jax.numpy as jnp
from jax import lax

PSIDE = 256
PATCH_DEV = 2
STEPS = 6
CLASSES = 16
PASSES = 4
NDEV = 32
PATCHES = 64
MAP_R = 1024
MAP_C = 2048
N_STORM = 16
N_TILE = 2


def draw_live_counts(key, part):
    pair_count = N_STORM // 2 * N_TILE
    lower_half = jax.random.randint(jax.random.fold_in(key, 7), (pair_count,), 0, PATCH_DEV + 1)
    forced = jax.random.randint(jax.random.fold_in(key, 17), (), 0, pair_count)
    lower_half = jnp.where(jnp.arange(pair_count, dtype=jnp.int32) == forced, 0, lower_half)
    lower_half = lower_half.reshape(N_STORM // 2, N_TILE)
    return jnp.concatenate([lower_half, PATCH_DEV - lower_half], axis=0).reshape(NDEV).astype(jnp.int32)


def draw_row_offset(key, part):
    half_rows = MAP_R // 2
    jitter_most = min(PSIDE // 2, half_rows - PSIDE)
    anchors = jax.random.randint(jax.random.fold_in(key, 11), (NDEV, 2), 0, half_rows - PSIDE - jitter_most + 1)
    jitters = jax.random.randint(jax.random.fold_in(key, 13), (NDEV, PATCH_DEV), 0, jitter_most + 1)
    position = jnp.arange(PATCH_DEV, dtype=jnp.int32)
    which_half = (position >= PATCH_DEV // 2).astype(jnp.int32)
    chosen = jnp.where(which_half[None, :] == 1, anchors[:, 1:2], anchors[:, 0:1])
    offsets = which_half[None, :] * half_rows + chosen + jitters
    return offsets.reshape(NDEV * PATCH_DEV).astype(jnp.int32)


def plant(result, rng, smallest, high):
    dims = result.shape
    index_at = [jax.random.randint(jax.random.fold_in(rng, axis), (), 0, dims[axis]) for axis in range(len(dims))]
    result = result.at[tuple(index_at)].set(smallest)
    longest = dims.index(max(dims))
    index_at[longest] = (index_at[longest] + 1) % dims[longest]
    return result.at[tuple(index_at)].set(high)


def shard_levels(own_key, dims, shards, low, largest):
    gain = 1.0
    for dim, blocks in shards:
        steps = jax.random.uniform(jax.random.fold_in(jax.random.fold_in(own_key, 6), dim), (blocks,), jnp.float32, low / len(shards), largest / len(shards))
        gain = gain * jnp.repeat(jnp.exp(steps), dims[dim] // blocks).reshape((-1,) + (1,) * (len(dims) - 1 - dim))
    return gain


def scatter_about(stream_key, shape, spread, most, shards=(), held_as=jnp.bfloat16):
    drawn = spread * jax.random.normal(stream_key, shape, jnp.float32)
    if shards:
        drawn = drawn * shard_levels(stream_key, shape, shards, -0.22, 0.18)
    return jnp.clip(drawn, -most, most).astype(held_as)


def setup_inputs(seed: int = 0, part: int = 0) -> dict:
    seeds = jax.random.split(jax.random.key(seed), 8)
    own_keys = jax.random.split(jax.random.fold_in(seeds[7], part), 8)
    patches = scatter_about(own_keys[0], (PATCHES, 2, PSIDE, PSIDE), 1.0, 4.0, ((0, 32),), jnp.float32)
    patch_coeffs = jnp.clip(jnp.exp(math.log(0.15) - 2.7080503 * jax.random.uniform(own_keys[1], (PATCHES, 2), jnp.float32) ** shard_levels(own_keys[1], (PATCHES, 2), ((0, 32),), -0.2, 0.2)), 0.01, 0.15)
    row_offset = draw_row_offset(jax.random.fold_in(jax.random.fold_in(seeds[7], part), 71), part)
    col_offset = plant(jax.random.randint(own_keys[3], (PATCHES,), 0, MAP_C - PSIDE + 1), jax.random.fold_in(own_keys[3], 1), 0, MAP_C - PSIDE).astype(jnp.int32)
    live_counts = draw_live_counts(jax.random.fold_in(jax.random.fold_in(seeds[7], part), 71), part)
    class_map = plant(jax.random.randint(own_keys[5], (MAP_R, MAP_C), 0, CLASSES), jax.random.fold_in(own_keys[5], 1), 0, CLASSES - 1).astype(jnp.int32)
    roughness = jnp.clip(jax.random.uniform(seeds[6], (CLASSES,), jnp.float32, 0.2, 0.9), 0.2, 0.9)
    return dict(patches=patches, patch_coeffs=patch_coeffs, row_offset=row_offset, col_offset=col_offset, live_counts=live_counts, class_map=class_map, roughness=roughness)


def neighbours(grid_in):
    padded = jnp.pad(grid_in, ((0, 0), (1, 1), (1, 1)))
    return padded[:, 2:, 1:-1] + padded[:, :-2, 1:-1] + padded[:, 1:-1, 2:] + padded[:, 1:-1, :-2] - 4.0 * grid_in

def advance(fields, coeffs):
    eastward = fields[:, 0]
    northward = fields[:, 1]
    drag_rate = coeffs[:, 0][:, None, None]
    turn_rate = coeffs[:, 1][:, None, None]
    for repeat in range(STEPS):
        wind_speed = jnp.sqrt(eastward * eastward + northward * northward + 0.25)
        eastward, northward = (eastward + 0.2 * neighbours(eastward) - drag_rate * wind_speed * eastward + turn_rate * northward, northward + 0.2 * neighbours(northward) - drag_rate * wind_speed * northward - turn_rate * eastward)
    return jnp.sqrt(eastward * eastward + northward * northward + 0.25)

def smooth_pass(padded, weights):
    centre = padded[1:-1, 1:-1]
    beside_all = padded[2:, 1:-1] + padded[:-2, 1:-1] + padded[1:-1, 2:] + padded[1:-1, :-2]
    return (1.0 - weights) * centre + weights * 0.25 * beside_all

def lookup(class_map, roughness):
    weights = jnp.zeros(class_map.shape, jnp.float32)
    for level in range(CLASSES):
        weights = weights + jnp.where(class_map == level, roughness[level], 0.0)
    return weights

def reference(patches, patch_coeffs, row_offset, col_offset, live_counts, class_map, roughness):
    slot_index = jnp.arange(PATCHES, dtype=jnp.int32)
    live = slot_index % PATCH_DEV < jnp.repeat(live_counts, PATCH_DEV)

    def block_gust(inputs):
        return advance(inputs[0], inputs[1])
    gusts = lax.map(block_gust, (patches.reshape(NDEV, PATCH_DEV, 2, PSIDE, PSIDE), patch_coeffs.reshape(NDEV, PATCH_DEV, 2)))
    gusts = gusts.reshape(PATCHES, PSIDE, PSIDE)
    gusts = jnp.where(live[:, None, None], gusts, 0.0).astype(jnp.bfloat16)

    def stamp(canvas, item):
        gust, row_start, col_start = item
        corner = (row_start.astype(jnp.int32), col_start.astype(jnp.int32))
        current = lax.dynamic_slice(canvas, corner, (PSIDE, PSIDE))
        return (lax.dynamic_update_slice(canvas, jnp.maximum(current, gust), corner), None)
    canvas, unused = lax.scan(stamp, jnp.zeros((MAP_R, MAP_C), jnp.bfloat16), (gusts, row_offset, col_offset))
    weights = lookup(class_map, roughness)
    smoothed = canvas.astype(jnp.float32)
    for repeat in range(PASSES):
        smoothed = smooth_pass(jnp.pad(smoothed, 1), weights)
    return smoothed
```

```python
import functools

import jax
import jax.numpy as jnp
from jax import lax
from jax.experimental import pallas as pl
from jax.experimental.pallas import tpu as pltpu
from jax.sharding import PartitionSpec as P

STEPS = 6
CLASSES = 16
PASSES = 4
HALO = 8
LANES = 128
F32 = jnp.float32
BF16 = jnp.bfloat16


def speed(e, n):
    return jnp.sqrt(e * e + n * n + 0.25)


def advance_into(source, slot, drag, turn, bufs, gust, lead, shift, side):
    chunk = 16
    pad = HALO
    for field in range(2):
        bufs[0][field, pad : pad + side, :] = source[slot, field]
    lane = lax.broadcasted_iota(jnp.int32, (chunk, side), 1)
    first = lane == 0
    last = lane == side - 1

    def across(v):
        left = jnp.where(first, 0.0, pltpu.roll(v, 1, 1))
        right = jnp.where(last, 0.0, pltpu.roll(v, side - 1, 1))
        return left + right

    for step in range(STEPS):
        src, dst = bufs[step % 2], bufs[(step + 1) % 2]
        for row in range(0, side, chunk):
            at = pad + row
            e = src[0, at : at + chunk, :]
            n = src[1, at : at + chunk, :]
            keep = 0.2 - drag * speed(e, n)
            around_e = src[0, at - 1 : at - 1 + chunk, :] + src[0, at + 1 : at + 1 + chunk, :] + across(e)
            around_n = src[1, at - 1 : at - 1 + chunk, :] + src[1, at + 1 : at + 1 + chunk, :] + across(n)
            e_new = e * keep + 0.2 * around_e + turn * n
            n_new = n * keep + 0.2 * around_n - turn * e
            if step + 1 < STEPS:
                dst[0, at : at + chunk, :] = e_new
                dst[1, at : at + chunk, :] = n_new
            else:
                gust[lead + row : lead + row + chunk, :] = pltpu.roll(speed(e_new, n_new), shift, 1)


def slabs_kernel(blocks, rows_dev, row_off, col_off, counts, coeffs, patches, out, buf_a, buf_b, gusts):
    side = patches.shape[3]
    window = rows_dev + 2 * HALO
    for buf in (buf_a, buf_b):
        for field in range(2):
            buf[field, 0:HALO, :] = jnp.zeros((HALO, side), F32)
            buf[field, HALO + side :, :] = jnp.zeros((HALO, side), F32)
    for slot in range(2):
        live = counts[0] > slot
        gusts[slot, 0:window, :] = jnp.zeros((window, side), F32)
        gusts[slot, window + side :, :] = jnp.zeros((window + HALO, side), F32)

        @pl.when(live)
        def _():
            advance_into(
                patches,
                slot,
                coeffs[slot, 0],
                coeffs[slot, 1],
                (buf_a, buf_b),
                gusts.at[slot],
                window,
                lax.rem(col_off[slot], side),
                side,
            )
            body = slice(window, window + side + HALO)
            gusts[slot, body, :] = pltpu.roll(gusts[slot, body, :], lax.rem(row_off[slot], HALO), 0)

        @pl.when(jnp.logical_not(live))
        def _():
            gusts[slot, window : window + side, :] = jnp.zeros((side, side), F32)

    row = lax.broadcasted_iota(jnp.int32, (HALO, side), 0)
    lane = lax.broadcasted_iota(jnp.int32, (HALO, side), 1)
    place = []
    for slot in range(2):
        major = lax.div(col_off[slot], side)
        minor = col_off[slot] - major * side
        place.append((jnp.full((HALO, side), major.astype(F32)), jnp.where(lane >= minor, 1.0, 0.0)))

    def start(slot, block):
        base = lax.div(row_off[slot], HALO) * HALO
        at = jnp.clip(block * rows_dev - HALO - base, -window, side + HALO) + window
        return pl.multiple_of(at, HALO)

    half = blocks // 2
    for block in range(blocks):
        main = 0 if block < half else 1
        other = 1 - main
        at = start(main, block)
        head = gusts[main, pl.ds(at, HALO), :]
        body = gusts[main, pl.ds(pl.multiple_of(at + HALO, HALO), rows_dev), :]
        tail = gusts[main, pl.ds(pl.multiple_of(at + HALO + rows_dev, HALO), HALO), :]
        if block == half - 1:
            tail = gusts[other, pl.ds(pl.multiple_of(start(other, block) + HALO + rows_dev, HALO), HALO), :]
        if block == half:
            head = gusts[other, pl.ds(start(other, block), HALO), :]
        head = jnp.where(row == 0, place[main][0], head)
        head = jnp.where(row == 1, place[main][1], head)
        head = jnp.where(row == 2, place[other][0], head)
        head = jnp.where(row == 3, place[other][1], head)
        out[block] = jnp.concatenate([head, body, tail], axis=0).astype(out.dtype)


def make_slabs(patches, coeffs, row_off, col_off, counts, blocks, rows_dev):
    side = patches.shape[3]
    window = rows_dev + 2 * HALO
    smem = pl.BlockSpec(memory_space=pltpu.SMEM)
    vmem = pl.BlockSpec(memory_space=pltpu.VMEM)
    return pl.pallas_call(
        functools.partial(slabs_kernel, blocks, rows_dev),
        name="slabs",
        out_shape=jax.ShapeDtypeStruct((blocks, window, side), BF16),
        in_specs=[smem, smem, smem, smem, vmem],
        out_specs=vmem,
        scratch_shapes=[
            pltpu.VMEM((2, side + 2 * HALO, side), F32),
            pltpu.VMEM((2, side + 2 * HALO, side), F32),
            pltpu.VMEM((2, side + 2 * window + HALO, side), F32),
        ],
        cost_estimate=pl.CostEstimate(flops=40 * STEPS * patches.size // 2, bytes_accessed=2 * patches.size, transcendentals=0),
    )(row_off, col_off, counts, coeffs, patches)


def stamp_kernel(cols_dev, map_cols, where, items, keep, give, strip):
    window, side = items.shape[1], items.shape[2]
    strip[...] = jnp.zeros_like(strip)
    upper_edge = where[1] == 1
    lower_edge = where[2] == 1
    tail_row = window - HALO
    cut = cols_dev + 2 * LANES

    def put(at, rows, value, mask):
        zero = jnp.zeros_like(value)
        col = pl.multiple_of(LANES + at * side, LANES)
        lo = (slice(rows, rows + value.shape[0]), pl.ds(col, side))
        hi = (slice(rows, rows + value.shape[0]), pl.ds(pl.multiple_of(col + side, LANES), side))
        strip[lo] = jnp.maximum(strip[lo], jnp.where(mask, value, zero))
        strip[hi] = jnp.maximum(strip[hi], jnp.where(mask, zero, value))

    for item in range(items.shape[0]):
        slab = items[item].astype(F32)
        head, body, tail = slab[0:HALO], slab[HALO:tail_row], slab[tail_row:]
        at = jnp.max(head[0:1, 0:LANES]).astype(jnp.int32)
        mask = head[1:2, :] > 0.5
        head_main = jnp.where(lower_edge, 0.0, head)
        tail_main = jnp.where(upper_edge, 0.0, tail)
        put(at, 0, jnp.concatenate([head_main, body, tail_main], axis=0), mask)

        @pl.when(upper_edge | lower_edge)
        def _():
            at_other = jnp.max(head[2:3, 0:LANES]).astype(jnp.int32)
            mask_other = head[3:4, :] > 0.5
            put(at_other, 0, head - head_main, mask_other)
            put(at_other, tail_row, tail - tail_main, mask_other)

    own = pl.multiple_of(where[0] * cols_dev, LANES)
    away = pl.multiple_of((1 - where[0]) * cols_dev, LANES)
    keep[...] = strip[:, pl.ds(own, cut)].astype(keep.dtype)
    give[...] = strip[:, pl.ds(away, cut)].astype(give.dtype)


def stamp(items, where, cols_dev, map_cols):
    window, side = items.shape[1], items.shape[2]
    cut = cols_dev + 2 * LANES
    smem = pl.BlockSpec(memory_space=pltpu.SMEM)
    vmem = pl.BlockSpec(memory_space=pltpu.VMEM)
    return pl.pallas_call(
        functools.partial(stamp_kernel, cols_dev, map_cols),
        name="stamp",
        out_shape=(jax.ShapeDtypeStruct((window, cut), BF16), jax.ShapeDtypeStruct((window, cut), BF16)),
        in_specs=[smem, vmem],
        out_specs=(vmem, vmem),
        scratch_shapes=[pltpu.VMEM((window, map_cols + 2 * LANES + side), F32)],
    )(where, items)


def blend_kernel(where, roughness, classes, above, below, beside, share):
    rows_dev, cols_dev = classes.shape
    tile = where[0]
    left = tile == 0

    def lookup(ids):
        weights = jnp.full(ids.shape, roughness[0])
        for level in range(1, CLASSES):
            weights = jnp.where(ids == float(level), roughness[level], weights)
        return 0.25 * weights

    inner = (HALO, HALO + rows_dev)
    has_above = where[3] == 1
    has_below = where[4] == 1
    mid = slice(LANES, LANES + cols_dev)
    edge = lookup(beside[...].astype(F32))
    row = lax.broadcasted_iota(jnp.int32, edge.shape, 0)
    bad = ((row < inner[0]) & jnp.logical_not(has_above)) | ((row >= inner[1]) & jnp.logical_not(has_below))
    edge = jnp.where(bad, 0.0, edge)
    share[:, 0:LANES] = jnp.where(left, 0.0, edge)
    share[:, LANES + cols_dev :] = jnp.where(left, edge, 0.0)
    share[0 : inner[0], mid] = jnp.where(has_above, lookup(above[...].astype(F32)), 0.0)
    share[inner[1] :, mid] = jnp.where(has_below, lookup(below[...].astype(F32)), 0.0)
    for at in range(0, rows_dev, 8):
        share[inner[0] + at : inner[0] + at + 8, mid] = lookup(classes[at : at + 8, :].astype(F32))


def smooth_kernel(where, keep, got, share, out, buf_a, buf_b):
    window, cut = keep.shape
    pad = HALO
    rows_dev, cols_dev = out.shape
    chunk = 8
    bufs = (buf_a, buf_b)
    for buf in bufs:
        buf[0:pad, :] = jnp.zeros((pad, cut), F32)
        buf[pad + window :, :] = jnp.zeros((pad, cut), F32)
    buf_a[pad : pad + window, :] = jnp.maximum(keep[...], got[...]).astype(F32)
    for step in range(PASSES):
        src, dst = bufs[step % 2], bufs[(step + 1) % 2]
        final = step + 1 == PASSES
        for row in range(HALO if final else 0, window - HALO if final else window, chunk):
            at = pad + row
            v = src[at : at + chunk, :]
            around = (
                src[at - 1 : at - 1 + chunk, :]
                + src[at + 1 : at + 1 + chunk, :]
                + pltpu.roll(v, 1, 1)
                + pltpu.roll(v, cut - 1, 1)
            )
            w = share[row : row + chunk, :]
            new = v - 4.0 * w * v + w * around
            if final:
                out[row - HALO : row - HALO + chunk, :] = new[:, LANES : LANES + cols_dev]
            else:
                dst[at : at + chunk, :] = jnp.where(w > 0.0, new, 0.0)


def on_device(patches, patch_coeffs, row_offset, col_offset, live_counts, class_map, roughness):
    storms = lax.axis_size("storm")
    rows_dev, cols_dev = class_map.shape
    tiles = lax.axis_size("tile")
    map_cols = cols_dev * tiles
    smem = pl.BlockSpec(memory_space=pltpu.SMEM)
    vmem = pl.BlockSpec(memory_space=pltpu.VMEM)
    side = patches.shape[3]
    window = rows_dev + 2 * HALO
    cut = cols_dev + 2 * LANES
    s = lax.axis_index("storm")
    t = lax.axis_index("tile")
    where = jnp.stack([t, s == storms // 2 - 1, s == storms // 2, s > 0, s < storms - 1]).astype(jnp.int32)

    slabs = make_slabs(patches, patch_coeffs, row_offset, col_offset, live_counts, storms, rows_dev)
    items = lax.all_to_all(slabs, "storm", split_axis=0, concat_axis=0, tiled=True)

    ids = class_map.astype(BF16)
    up = [(i + 1, i) for i in range(storms - 1)]
    down = [(i, i + 1) for i in range(storms - 1)]
    above = lax.ppermute(ids[rows_dev - HALO :], "storm", down)
    below = lax.ppermute(ids[:HALO], "storm", up)
    edge_col = jnp.where(t == 0, cols_dev - LANES, 0)
    tall = jnp.concatenate([above, ids, below], axis=0)
    beside = lax.ppermute(
        lax.dynamic_slice_in_dim(tall, edge_col, LANES, 1), "tile", [(0, 1), (1, 0)]
    )
    share = pl.pallas_call(
        blend_kernel,
        name="blend",
        out_shape=jax.ShapeDtypeStruct((window, cut), F32),
        in_specs=[smem, smem, vmem, vmem, vmem, vmem],
        out_specs=vmem,
    )(where, roughness, class_map, above, below, beside)

    items, share = lax.optimization_barrier((items, share))
    keep, give = stamp(items, where, cols_dev, map_cols)
    got = lax.ppermute(give, "tile", [(0, 1), (1, 0)])
    return pl.pallas_call(
        smooth_kernel,
        name="smooth",
        out_shape=jax.ShapeDtypeStruct((rows_dev, cols_dev), F32),
        in_specs=[smem, vmem, vmem, vmem],
        out_specs=vmem,
        scratch_shapes=[pltpu.VMEM((window + 2 * HALO, cut), F32)] * 2,
    )(where, keep, got, share)


def solution(mesh):
    return jax.shard_map(
        on_device,
        mesh=mesh,
        in_specs=(
            P(("grp", "storm", "tile"), None, None, None),
            P(("grp", "storm", "tile"), None),
            P(("grp", "storm", "tile")),
            P(("grp", "storm", "tile")),
            P(("grp", "storm", "tile")),
            P(("grp", "storm"), "tile"),
            P(),
        ),
        out_specs=P(("grp", "storm"), "tile"),
        check_vma=False,
    )
```

```python
import functools

import jax
import jax.numpy as jnp
from jax import lax
from jax.experimental import pallas as pl
from jax.experimental.pallas import tpu as pltpu
from jax.sharding import PartitionSpec as P

STEPS = 6
CLASSES = 16
PASSES = 4
HALO = 8
LANES = 128
SMALL = pltpu.CompilerParams(vmem_limit_bytes=16 * 1024 * 1024)
F32 = jnp.float32
BF16 = jnp.bfloat16


def spread(side):
    column = lax.broadcasted_iota(jnp.int32, (side, side), 0)
    place = lax.broadcasted_iota(jnp.int32, (side, side), 1)
    parts = side // LANES
    return jnp.where(column == parts * lax.rem(place, LANES) + lax.div(place, LANES), 1.0, 0.0).astype(BF16)


def gather_turned(side, turn):
    place = lax.broadcasted_iota(jnp.int32, (side, side), 0)
    column = lax.broadcasted_iota(jnp.int32, (side, side), 1)
    parts = side // LANES
    moved = parts * lax.rem(place, LANES) + lax.div(place, LANES) + turn
    moved = jnp.where(moved >= side, moved - side, moved)
    return jnp.where(column == moved, 1.0, 0.0).astype(BF16)


def select_columns(x, one_hot):
    total = None
    for term in range(3):
        piece = x.astype(BF16)
        product = jnp.dot(piece, one_hot, preferred_element_type=F32)
        total = product if total is None else total + product
        if term < 2:
            x = x - piece.astype(F32)
    return total


def advance_into(source, drag, turn, bufs, gust, lead, side):
    tiles = side // HALO + 1
    count = side // LANES
    lane = lax.broadcasted_iota(jnp.int32, (HALO, LANES), 1)
    row = lax.broadcasted_iota(jnp.int32, (HALO, LANES), 0)
    first, last = lane == 0, lane == LANES - 1
    parts = [slice(c * LANES, (c + 1) * LANES) for c in range(count)]

    def sides(v):
        before = [jnp.where(first, 0.0, pltpu.roll(v[-1], 1, 1))] + v[:-1]
        after = v[1:] + [jnp.where(last, 0.0, pltpu.roll(v[0], LANES - 1, 1))]
        return [x + y for x, y in zip(before, after)]

    def put(buf, field, k, c, v):
        if k + (HALO - 1) * tiles >= side:
            v = jnp.where(row == HALO - 1, 0.0, v)
        buf[field, k + 1, :, parts[c]] = v
        if k == tiles - 1:
            buf[field, 0, :, parts[c]] = jnp.where(row == 0, 0.0, pltpu.roll(v, 1, 0))
        if k == 0:
            buf[field, tiles + 1, :, parts[c]] = jnp.where(row == HALO - 1, 0.0, pltpu.roll(v, HALO - 1, 0))

    for field in range(2):
        for k in range(tiles):
            for c in range(count):
                put(bufs[0], field, k, c, source[field, c, pl.ds(k, HALO, stride=tiles), :])
    turn = 5.0 * turn
    for step in range(STEPS):
        src, dst = bufs[step % 2], bufs[(step + 1) % 2]
        scale = 0.2**step
        pull = drag * (5.0 * scale)
        for k in range(tiles):
            e = [src[0, k + 1, :, p] for p in parts]
            n = [src[1, k + 1, :, p] for p in parts]
            side_e, side_n = sides(e), sides(n)
            for c, p in enumerate(parts):
                power = e[c] * e[c] + n[c] * n[c] + 0.25 / scale**2
                keep = 1.0 - pull * (power * lax.rsqrt(power))
                around_e = (src[0, k, :, p] + src[0, k + 2, :, p]) + side_e[c]
                around_n = (src[1, k, :, p] + src[1, k + 2, :, p]) + side_n[c]
                e_new = around_e + e[c] * keep + turn * n[c]
                n_new = around_n + n[c] * keep - turn * e[c]
                if step + 1 < STEPS:
                    put(dst, 0, k, c, e_new)
                    put(dst, 1, k, c, n_new)
                else:
                    power = e_new * e_new + n_new * n_new + 0.25 / (0.2 * scale) ** 2
                    v = (0.2 * scale) * (power * lax.rsqrt(power))
                    if k + (HALO - 1) * tiles >= side:
                        v = jnp.where(row == HALO - 1, 0.0, v)
                    gust[c, pl.ds(lead + k, HALO, stride=tiles), :] = v


def slabs_kernel(blocks, rows_dev, row_off, col_off, counts, coeffs, patches, out, loaded, buf_a, buf_b, gusts, sems):
    side = patches.shape[3]
    parts = side // LANES
    window = rows_dev + 2 * HALO

    def fetch(slot):
        return [
            pltpu.make_async_copy(
                patches.at[slot, field, :, pl.ds(c * LANES, LANES)],
                loaded.at[slot, field, c, pl.ds(0, side), :],
                sems.at[slot, field, c],
            )
            for field in range(2)
            for c in range(parts)
        ]

    for slot in range(2):

        @pl.when(counts[0] > slot)
        def _():
            for copy in fetch(slot):
                copy.start()

        loaded[slot, :, :, side:, :] = jnp.zeros((2, parts, HALO, LANES), F32)
        gusts[slot, :, 0:window, :] = jnp.zeros((parts, window, LANES), F32)
        gusts[slot, :, window + side :, :] = jnp.zeros((parts, window + HALO, LANES), F32)

    for slot in range(2):
        live = counts[0] > slot

        @pl.when(live)
        def _():
            for copy in fetch(slot):
                copy.wait()
            gusts[slot, :, window : window + HALO, :] = jnp.zeros((parts, HALO, LANES), F32)
            one_hot = spread(side)
            for field in range(2):
                both = jnp.concatenate([loaded[slot, field, c, 0:side, :] for c in range(parts)], axis=1)
                both = select_columns(both, one_hot)
                for c in range(parts):
                    loaded[slot, field, c, 0:side, :] = both[:, c * LANES : (c + 1) * LANES]
            advance_into(
                loaded.at[slot],
                coeffs[slot, 0],
                coeffs[slot, 1],
                (buf_a, buf_b),
                gusts.at[slot],
                window + lax.rem(row_off[slot], HALO),
                side,
            )
            body = slice(window, window + side + HALO)
            both = jnp.concatenate([gusts[slot, c, body, :] for c in range(parts)], axis=1).astype(BF16)
            both = jnp.dot(both, gather_turned(side, lax.rem(col_off[slot], side)), preferred_element_type=F32)
            for c in range(parts):
                gusts[slot, c, body, :] = both[:, c * LANES : (c + 1) * LANES]

        @pl.when(jnp.logical_not(live))
        def _():
            gusts[slot, :, window : window + side, :] = jnp.zeros((parts, side, LANES), F32)

    row = lax.broadcasted_iota(jnp.int32, (HALO, side), 0)
    lane = lax.broadcasted_iota(jnp.int32, (HALO, side), 1)
    place = []
    for slot in range(2):
        major = lax.div(col_off[slot], side)
        minor = col_off[slot] - major * side
        place.append((jnp.full((HALO, side), major.astype(F32)), jnp.where(lane >= minor, 1.0, 0.0)))

    def rows(slot, block, skip, count):
        base = lax.div(row_off[slot], HALO) * HALO
        at = jnp.clip(block * rows_dev - HALO - base, -window, side + HALO) + window + skip
        at = pl.ds(pl.multiple_of(at, HALO), count)
        return jnp.concatenate([gusts[slot, c, at, :] for c in range(parts)], axis=1)

    half = blocks // 2
    for block in range(blocks):
        main = 0 if block < half else 1
        other = 1 - main
        head = rows(other if block == half else main, block, 0, HALO)
        body = rows(main, block, HALO, rows_dev)
        tail = rows(other if block == half - 1 else main, block, HALO + rows_dev, HALO)
        head = jnp.where(row == 0, place[main][0], head)
        head = jnp.where(row == 1, place[main][1], head)
        head = jnp.where(row == 2, place[other][0], head)
        head = jnp.where(row == 3, place[other][1], head)
        out[block] = jnp.concatenate([head, body, tail], axis=0).astype(out.dtype)


def make_slabs(patches, coeffs, row_off, col_off, counts, blocks, rows_dev):
    side = patches.shape[3]
    parts = side // LANES
    window = rows_dev + 2 * HALO
    smem = pl.BlockSpec(memory_space=pltpu.SMEM)
    vmem = pl.BlockSpec(memory_space=pltpu.VMEM)
    return pl.pallas_call(
        functools.partial(slabs_kernel, blocks, rows_dev),
        name="slabs",
        compiler_params=SMALL,
        out_shape=jax.ShapeDtypeStruct((blocks, window, side), BF16),
        in_specs=[smem, smem, smem, smem, pl.BlockSpec(memory_space=pl.ANY)],
        out_specs=vmem,
        scratch_shapes=[
            pltpu.VMEM((2, 2, parts, side + HALO, LANES), F32),
            pltpu.VMEM((2, side // HALO + 3, HALO, side), F32),
            pltpu.VMEM((2, side // HALO + 3, HALO, side), F32),
            pltpu.VMEM((2, parts, side + 2 * window + HALO, LANES), F32),
            pltpu.SemaphoreType.DMA((2, 2, parts)),
        ],
        cost_estimate=pl.CostEstimate(flops=40 * STEPS * patches.size // 2, bytes_accessed=2 * patches.size, transcendentals=0),
    )(row_off, col_off, counts, coeffs, patches)


def stamp_kernel(cols_dev, map_cols, where, items, keep, give, strip):
    window, side = items.shape[1], items.shape[2]
    strip[...] = jnp.zeros_like(strip)
    upper_edge = where[1] == 1
    lower_edge = where[2] == 1
    tail_row = window - HALO
    cut = cols_dev + 2 * LANES

    def put(at, rows, value, mask):
        zero = jnp.zeros_like(value)
        col = pl.multiple_of(LANES + at * side, LANES)
        lo = (slice(rows, rows + value.shape[0]), pl.ds(col, side))
        hi = (slice(rows, rows + value.shape[0]), pl.ds(pl.multiple_of(col + side, LANES), side))
        strip[lo] = jnp.maximum(strip[lo], jnp.where(mask, value, zero))
        strip[hi] = jnp.maximum(strip[hi], jnp.where(mask, zero, value))

    count = items.shape[0]

    def column(item, at):
        return items[item, 0:16, 0:LANES].astype(F32)[at, 0].astype(jnp.int32)

    columns = [column(item, 0) for item in range(count)]
    for item in range(count):
        slab = items[item].astype(F32)
        head, body, tail = slab[0:HALO], slab[HALO:tail_row], slab[tail_row:]
        head = jnp.where(lower_edge, 0.0, head)
        tail = jnp.where(upper_edge, 0.0, tail)
        mask = slab[1:2, :] > 0.5
        put(columns[item], 0, jnp.concatenate([head, body, tail], axis=0), mask)

    def other(rows):
        columns = [column(item, 2) for item in range(count)]
        for item in range(count):
            mask = items[item, 0:HALO, :].astype(F32)[3:4, :] > 0.5
            put(columns[item], rows, items[item, rows : rows + HALO, :].astype(F32), mask)

    pl.when(lower_edge)(lambda: other(0))
    pl.when(upper_edge)(lambda: other(tail_row))

    own = pl.multiple_of(where[0] * cols_dev, LANES)
    away = pl.multiple_of((1 - where[0]) * cols_dev, LANES)
    keep[...] = strip[:, pl.ds(own, cut)].astype(keep.dtype)
    give[...] = strip[:, pl.ds(away, cut)].astype(give.dtype)


def stamp(items, where, cols_dev, map_cols):
    window, side = items.shape[1], items.shape[2]
    cut = cols_dev + 2 * LANES
    smem = pl.BlockSpec(memory_space=pltpu.SMEM)
    vmem = pl.BlockSpec(memory_space=pltpu.VMEM)
    return pl.pallas_call(
        functools.partial(stamp_kernel, cols_dev, map_cols),
        name="stamp",
        compiler_params=SMALL,
        out_shape=(jax.ShapeDtypeStruct((window, cut), BF16), jax.ShapeDtypeStruct((window, cut), BF16)),
        in_specs=[smem, vmem],
        out_specs=(vmem, vmem),
        scratch_shapes=[pltpu.VMEM((window, map_cols + 2 * LANES + side), F32)],
    )(where, items)


def blend_kernel(where, roughness, classes, above, below, beside, share):
    rows_dev, cols_dev = classes.shape
    tile = where[0]
    left = tile == 0

    def lookup(ids):
        weights = jnp.full(ids.shape, roughness[0])
        for level in range(1, CLASSES):
            weights = jnp.where(ids == float(level), roughness[level], weights)
        return 0.25 * weights

    inner = (HALO, HALO + rows_dev)
    has_above = where[3] == 1
    has_below = where[4] == 1
    mid = slice(LANES, LANES + cols_dev)
    edge = lookup(beside[...].astype(F32))
    row = lax.broadcasted_iota(jnp.int32, edge.shape, 0)
    bad = ((row < inner[0]) & jnp.logical_not(has_above)) | ((row >= inner[1]) & jnp.logical_not(has_below))
    edge = jnp.where(bad, 0.0, edge)
    share[:, 0:LANES] = jnp.where(left, 0.0, edge)
    share[:, LANES + cols_dev :] = jnp.where(left, edge, 0.0)
    share[0 : inner[0], mid] = jnp.where(has_above, lookup(above[...].astype(F32)), 0.0)
    share[inner[1] :, mid] = jnp.where(has_below, lookup(below[...].astype(F32)), 0.0)
    for at in range(0, rows_dev, 8):
        share[inner[0] + at : inner[0] + at + 8, mid] = lookup(classes[at : at + 8, :].astype(F32))


def smooth_kernel(where, keep, got, share, out, buf_a, buf_b):
    window, cut = keep.shape
    pad = HALO
    rows_dev, cols_dev = out.shape
    chunk = 8
    bufs = (buf_a, buf_b)
    for buf in bufs:
        buf[0:pad, :] = jnp.zeros((pad, cut), F32)
        buf[pad + window :, :] = jnp.zeros((pad, cut), F32)
    buf_a[pad : pad + window, :] = jnp.maximum(keep[...], got[...]).astype(F32)
    for step in range(PASSES):
        src, dst = bufs[step % 2], bufs[(step + 1) % 2]
        final = step + 1 == PASSES
        for row in range(HALO if final else 0, window - HALO if final else window, chunk):
            at = pad + row
            v = src[at : at + chunk, :]
            around = (
                src[at - 1 : at - 1 + chunk, :]
                + src[at + 1 : at + 1 + chunk, :]
                + pltpu.roll(v, 1, 1)
                + pltpu.roll(v, cut - 1, 1)
            )
            w = share[row : row + chunk, :]
            new = v - 4.0 * w * v + w * around
            if final:
                out[row - HALO : row - HALO + chunk, :] = new[:, LANES : LANES + cols_dev]
            else:
                dst[at : at + chunk, :] = jnp.where(w > 0.0, new, 0.0)


def on_device(patches, patch_coeffs, row_offset, col_offset, live_counts, class_map, roughness):
    storms = lax.axis_size("storm")
    rows_dev, cols_dev = class_map.shape
    tiles = lax.axis_size("tile")
    map_cols = cols_dev * tiles
    smem = pl.BlockSpec(memory_space=pltpu.SMEM)
    vmem = pl.BlockSpec(memory_space=pltpu.VMEM)
    side = patches.shape[3]
    window = rows_dev + 2 * HALO
    cut = cols_dev + 2 * LANES
    s = lax.axis_index("storm")
    t = lax.axis_index("tile")
    where = jnp.stack([t, s == storms // 2 - 1, s == storms // 2, s > 0, s < storms - 1]).astype(jnp.int32)

    slabs = make_slabs(patches, patch_coeffs, row_offset, col_offset, live_counts, storms, rows_dev)
    items = lax.all_to_all(slabs, "storm", split_axis=0, concat_axis=0, tiled=True)

    ids = class_map.astype(BF16)
    up = [(i + 1, i) for i in range(storms - 1)]
    down = [(i, i + 1) for i in range(storms - 1)]
    above = lax.ppermute(ids[rows_dev - HALO :], "storm", down)
    below = lax.ppermute(ids[:HALO], "storm", up)
    edge_col = jnp.where(t == 0, cols_dev - LANES, 0)
    tall = jnp.concatenate([above, ids, below], axis=0)
    beside = lax.ppermute(
        lax.dynamic_slice_in_dim(tall, edge_col, LANES, 1), "tile", [(0, 1), (1, 0)]
    )
    share = pl.pallas_call(
        blend_kernel,
        name="blend",
        compiler_params=SMALL,
        out_shape=jax.ShapeDtypeStruct((window, cut), F32),
        in_specs=[smem, smem, vmem, vmem, vmem, vmem],
        out_specs=vmem,
    )(where, roughness, class_map, above, below, beside)

    items, share = lax.optimization_barrier((items, share))
    keep, give = stamp(items, where, cols_dev, map_cols)
    got = lax.ppermute(give, "tile", [(0, 1), (1, 0)])
    return pl.pallas_call(
        smooth_kernel,
        name="smooth",
        compiler_params=SMALL,
        out_shape=jax.ShapeDtypeStruct((rows_dev, cols_dev), F32),
        in_specs=[smem, vmem, vmem, vmem],
        out_specs=vmem,
        scratch_shapes=[pltpu.VMEM((window + 2 * HALO, cut), F32)] * 2,
    )(where, keep, got, share)


def solution(mesh):
    return jax.shard_map(
        on_device,
        mesh=mesh,
        in_specs=(
            P(("grp", "storm", "tile"), None, None, None),
            P(("grp", "storm", "tile"), None),
            P(("grp", "storm", "tile")),
            P(("grp", "storm", "tile")),
            P(("grp", "storm", "tile")),
            P(("grp", "storm"), "tile"),
            P(),
        ),
        out_specs=P(("grp", "storm"), "tile"),
        check_vma=False,
    )
```

```python
import functools

import jax
import jax.numpy as jnp
from jax import lax
from jax.experimental import pallas as pl
from jax.experimental.pallas import tpu as pltpu
from jax.sharding import PartitionSpec as P


STEPS = 6
CLASSES = 16
PASSES = 4
HALO = 8
LANES = 128
SEND_ROWS = 16
SMALL = pltpu.CompilerParams(vmem_limit_bytes=16 * 1024 * 1024)
F32 = jnp.float32
BF16 = jnp.bfloat16


def spread(side):
    column = lax.broadcasted_iota(jnp.int32, (side, side), 0)
    place = lax.broadcasted_iota(jnp.int32, (side, side), 1)
    parts = side // LANES
    return jnp.where(column == parts * lax.rem(place, LANES) + lax.div(place, LANES), 1.0, 0.0).astype(BF16)


def gather_turned(side, turn):
    place = lax.broadcasted_iota(jnp.int32, (side, side), 0)
    column = lax.broadcasted_iota(jnp.int32, (side, side), 1)
    parts = side // LANES
    moved = parts * lax.rem(place, LANES) + lax.div(place, LANES) + turn
    moved = jnp.where(moved >= side, moved - side, moved)
    return jnp.where(column == moved, 1.0, 0.0).astype(BF16)


def select_columns(x, one_hot):
    total = None
    for term in range(3):
        piece = x.astype(BF16)
        product = jnp.dot(piece, one_hot, preferred_element_type=F32)
        total = product if total is None else total + product
        if term < 2:
            x = x - piece.astype(F32)
    return total


def advance_into(source, drag, turn, bufs, gust, lead, side):
    tiles = side // HALO + 1
    count = side // LANES
    lane = lax.broadcasted_iota(jnp.int32, (HALO, LANES), 1)
    row = lax.broadcasted_iota(jnp.int32, (HALO, LANES), 0)
    first, last = lane == 0, lane == LANES - 1
    parts = [slice(c * LANES, (c + 1) * LANES) for c in range(count)]

    def sides(v):
        before = [jnp.where(first, 0.0, pltpu.roll(v[-1], 1, 1))] + v[:-1]
        after = v[1:] + [jnp.where(last, 0.0, pltpu.roll(v[0], LANES - 1, 1))]
        return [x + y for x, y in zip(before, after)]

    def put(buf, field, k, c, v):
        if k + (HALO - 1) * tiles >= side:
            v = jnp.where(row == HALO - 1, 0.0, v)
        buf[field, k + 1, :, parts[c]] = v
        if k == tiles - 1:
            buf[field, 0, :, parts[c]] = jnp.where(row == 0, 0.0, pltpu.roll(v, 1, 0))
        if k == 0:
            buf[field, tiles + 1, :, parts[c]] = jnp.where(row == HALO - 1, 0.0, pltpu.roll(v, HALO - 1, 0))

    for field in range(2):
        for k in range(tiles):
            for c in range(count):
                put(bufs[0], field, k, c, source[field, c, pl.ds(k, HALO, stride=tiles), :])
    turn = 5.0 * turn
    for step in range(STEPS):
        src, dst = bufs[step % 2], bufs[(step + 1) % 2]
        scale = 0.2**step
        pull = drag * (5.0 * scale)
        for k in range(tiles):
            e = [src[0, k + 1, :, p] for p in parts]
            n = [src[1, k + 1, :, p] for p in parts]
            side_e, side_n = sides(e), sides(n)
            for c, p in enumerate(parts):
                power = e[c] * e[c] + n[c] * n[c] + 0.25 / scale**2
                keep = 1.0 - pull * (power * lax.rsqrt(power))
                around_e = (src[0, k, :, p] + src[0, k + 2, :, p]) + side_e[c]
                around_n = (src[1, k, :, p] + src[1, k + 2, :, p]) + side_n[c]
                e_new = around_e + e[c] * keep + turn * n[c]
                n_new = around_n + n[c] * keep - turn * e[c]
                if step + 1 < STEPS:
                    put(dst, 0, k, c, e_new)
                    put(dst, 1, k, c, n_new)
                else:
                    power = e_new * e_new + n_new * n_new + 0.25 / (0.2 * scale) ** 2
                    v = (0.2 * scale) * (power * lax.rsqrt(power))
                    if k + (HALO - 1) * tiles >= side:
                        v = jnp.where(row == HALO - 1, 0.0, v)
                    gust[c, pl.ds(lead + k, HALO, stride=tiles), :] = v


def slabs_kernel(
    hops,
    rows_dev,
    counts,
    row_hbm,
    col_hbm,
    coeffs_hbm,
    classes,
    patches,
    own,
    give,
    row_off,
    col_off,
    coeffs,
    loaded,
    buf_a,
    buf_b,
    gusts,
    edges,
    sems,
    small_sems,
):
    smalls = [
        pltpu.make_async_copy(source, target, small_sems.at[i])
        for i, (source, target) in enumerate(
            (
                (row_hbm, row_off),
                (col_hbm, col_off),
                (coeffs_hbm, coeffs),
                (classes.at[pl.ds(0, HALO), :], edges.at[0]),
                (classes.at[pl.ds(rows_dev - HALO, HALO), :], edges.at[1]),
            )
        )
    ]
    for copy in smalls:
        copy.start()
    side = patches.shape[3]
    parts = side // LANES
    window = rows_dev + 2 * HALO
    half = len(hops)
    storm, tile = lax.axis_index("storm"), lax.axis_index("tile")

    def fetch(slot, field):
        return [
            pltpu.make_async_copy(
                patches.at[slot, field, :, pl.ds(c * LANES, LANES)],
                loaded.at[slot, field, c, pl.ds(0, side), :],
                sems.at[slot, field, c],
            )
            for c in range(parts)
        ]

    for slot in range(2):

        @pl.when(counts[0] > slot)
        def _():
            for field in range(2):
                for copy in fetch(slot, field):
                    copy.start()

    row = lax.broadcasted_iota(jnp.int32, (HALO, side), 0)
    lane = lax.broadcasted_iota(jnp.int32, (HALO, side), 1)
    for slot in range(2):
        loaded[slot, :, :, side:, :] = jnp.zeros((2, parts, loaded.shape[3] - side, LANES), F32)
        gusts[slot, :, 0:window, :] = jnp.zeros((parts, window, LANES), F32)
        gusts[slot, :, window + side :, :] = jnp.zeros((parts, window + HALO, LANES), F32)

    def rows(slot, block, skip, count):
        base = lax.div(row_off[slot], HALO) * HALO
        at = jnp.clip(block * rows_dev - HALO - base, -window, side + HALO) + window + skip
        at = pl.ds(pl.multiple_of(at, HALO), count)
        return jnp.concatenate([gusts[slot, c, at, :] for c in range(parts)], axis=1)

    def build(out, item, block):
        main = jnp.where(block < half, 0, 1)
        other = 1 - main
        head = rows(jnp.where(block == half, other, main), block, 0, HALO)
        body = rows(main, block, HALO, rows_dev)
        tail = rows(jnp.where(block == half - 1, other, main), block, HALO + rows_dev, HALO)
        for line, slot in ((0, main), (2, other)):
            major = lax.div(col_off[slot], side)
            minor = col_off[slot] - major * side
            head = jnp.where(row == line, major.astype(F32), head)
            head = jnp.where(row == line + 1, jnp.where(lane >= minor, 1.0, 0.0), head)
        out[item, 0:window, :] = jnp.concatenate([head, body, tail], axis=0).astype(out.dtype)
        lines = jnp.where(block == storm + 1, bottom, jnp.where(block == storm - 1, top, 0.0))
        out[item, window:, :] = lines.astype(out.dtype)

    for copy in smalls:
        copy.wait()
    for slot in range(2):
        live = counts[0] > slot

        @pl.when(live)
        def _():
            gusts[slot, :, window : window + HALO, :] = jnp.zeros((parts, HALO, LANES), F32)
            one_hot = spread(side)
            for field in range(2):
                for copy in fetch(slot, field):
                    copy.wait()
                both = jnp.concatenate([loaded[slot, field, c, 0:side, :] for c in range(parts)], axis=1)
                both = select_columns(both, one_hot)
                for c in range(parts):
                    loaded[slot, field, c, 0:side, :] = both[:, c * LANES : (c + 1) * LANES]
            advance_into(
                loaded.at[slot],
                coeffs[slot, 0],
                coeffs[slot, 1],
                (buf_a, buf_b),
                gusts.at[slot],
                window + lax.rem(row_off[slot], HALO),
                side,
            )
            body = slice(window, window + side + HALO)
            both = jnp.concatenate([gusts[slot, c, body, :] for c in range(parts)], axis=1).astype(BF16)
            both = jnp.dot(both, gather_turned(side, lax.rem(col_off[slot], side)), preferred_element_type=F32)
            for c in range(parts):
                gusts[slot, c, body, :] = both[:, c * LANES : (c + 1) * LANES]

        @pl.when(jnp.logical_not(live))
        def _():
            gusts[slot, :, window : window + side, :] = jnp.zeros((parts, side, LANES), F32)

    def folded(lines):
        lines = lines.astype(F32)
        return jnp.concatenate([lines[:, at : at + side] for at in range(0, lines.shape[1], side)], axis=0)

    top, bottom = folded(edges[0, 0:PASSES, :]), folded(edges[1, HALO - PASSES : HALO, :])
    for item, (a, b) in enumerate(hops):
        build(own, item, storm ^ jnp.where(tile == 0, a, b))
        build(give, item, storm ^ jnp.where(tile == 0, b, a))


def make_slabs(patches, coeffs, row_off, col_off, counts, classes, hops):
    side = patches.shape[3]
    parts = side // LANES
    rows_dev, cols_dev = classes.shape
    window = rows_dev + 2 * HALO
    hbm = pl.BlockSpec(memory_space=pltpu.HBM)
    vmem = pl.BlockSpec(memory_space=pltpu.VMEM)
    result = jax.ShapeDtypeStruct((len(hops), window + PASSES * cols_dev // side, side), BF16)
    return pl.pallas_call(
        functools.partial(slabs_kernel, hops, rows_dev),
        name="slabs",
        out_shape=(result, result),
        compiler_params=SMALL,
        in_specs=[pl.BlockSpec(memory_space=pltpu.SMEM)] + [hbm] * 5,
        out_specs=(vmem, vmem),
        scratch_shapes=[
            pltpu.SMEM(row_off.shape, row_off.dtype),
            pltpu.SMEM(col_off.shape, col_off.dtype),
            pltpu.SMEM(coeffs.shape, coeffs.dtype),
            pltpu.VMEM((2, 2, parts, side + side // HALO + HALO, LANES), F32),
            pltpu.VMEM((2, side // HALO + 3, HALO, side), F32),
            pltpu.VMEM((2, side // HALO + 3, HALO, side), F32),
            pltpu.VMEM((2, parts, side + 2 * window + HALO, LANES), F32),
            pltpu.VMEM((2, HALO, cols_dev), classes.dtype),
            pltpu.SemaphoreType.DMA((2, 2, parts)),
            pltpu.SemaphoreType.DMA((5,)),
        ],
        cost_estimate=pl.CostEstimate(flops=40 * STEPS * patches.size // 2, bytes_accessed=2 * patches.size, transcendentals=0),
    )(counts, *(pltpu.with_memory_space_constraint(x, pltpu.HBM) for x in (row_off, col_off, coeffs, classes, patches)))


def stamp_kernel(cols_dev, window, hops, *refs):
    arrived, (keep, give, strip) = refs[: len(hops)], refs[len(hops) :]
    items = [ref.at[part] for ref in arrived for part in range(ref.shape[0])]
    side = arrived[0].shape[2]
    strip[...] = jnp.zeros_like(strip)
    storm, tile = lax.axis_index("storm"), lax.axis_index("tile")
    storms = lax.axis_size("storm")
    upper_edge = storm == storms // 2 - 1
    lower_edge = storm == storms // 2
    tail_row = window - HALO
    cut = cols_dev + 2 * LANES

    def put(at, rows, value, mask):
        zero = jnp.zeros_like(value)
        col = pl.multiple_of(LANES + at * side, LANES)
        lo = (slice(rows, rows + value.shape[0]), pl.ds(col, side))
        hi = (slice(rows, rows + value.shape[0]), pl.ds(pl.multiple_of(col + side, LANES), side))
        strip[lo] = jnp.maximum(strip[lo], jnp.where(mask, value, zero))
        strip[hi] = jnp.maximum(strip[hi], jnp.where(mask, zero, value))

    count = len(items)

    def column(item, at):
        return items[item][0:16, 0:LANES].astype(F32)[at, 0].astype(jnp.int32)

    columns = [column(item, 0) for item in range(count)]
    for item in range(count):
        slab = items[item][0:window, :].astype(F32)
        head, body, tail = slab[0:HALO], slab[HALO:tail_row], slab[tail_row:]
        head = jnp.where(lower_edge, 0.0, head)
        tail = jnp.where(upper_edge, 0.0, tail)
        mask = slab[1:2, :] > 0.5
        put(columns[item], 0, jnp.concatenate([head, body, tail], axis=0), mask)

    def other(rows):
        columns = [column(item, 2) for item in range(count)]
        for item in range(count):
            mask = items[item][0:HALO, :].astype(F32)[3:4, :] > 0.5
            put(columns[item], rows, items[item][rows : rows + HALO, :].astype(F32), mask)

    pl.when(lower_edge)(lambda: other(0))
    pl.when(upper_edge)(lambda: other(tail_row))

    for item, (a, b) in enumerate(hops):
        source = storm ^ jnp.where(tile == 0, a, b)

        def lines(to):
            for part in range(arrived[item].shape[0]):
                values = arrived[item][part, window:, :].astype(F32)
                for fold in range(cols_dev // side):
                    at = LANES + jnp.where(tile == part, 0, cols_dev) + fold * side
                    at = pl.ds(pl.multiple_of(at, LANES), side)
                    strip[to : to + PASSES, at] = values[fold * PASSES : (fold + 1) * PASSES]

        pl.when(source == storm - 1)(lambda: lines(window + HALO - PASSES))
        pl.when(source == storm + 1)(lambda: lines(window + HALO))

    own = pl.multiple_of(tile * cols_dev, LANES)
    away = pl.multiple_of((1 - tile) * cols_dev, LANES)
    keep[...] = strip[:, pl.ds(own, cut)].astype(keep.dtype)
    give[...] = strip[:, pl.ds(away, cut)].astype(give.dtype)


def stamp(arrived, hops, rows_dev, cols_dev, map_cols):
    side = arrived[0].shape[2]
    window = rows_dev + 2 * HALO
    height = window + 2 * HALO
    cut = cols_dev + 2 * LANES
    vmem = pl.BlockSpec(memory_space=pltpu.VMEM)
    return pl.pallas_call(
        functools.partial(stamp_kernel, cols_dev, window, hops),
        name="stamp",
        compiler_params=SMALL,
        out_shape=(jax.ShapeDtypeStruct((height, cut), BF16), jax.ShapeDtypeStruct((height, cut), BF16)),
        in_specs=[vmem] * len(arrived),
        out_specs=(vmem, vmem),
        scratch_shapes=[pltpu.VMEM((height, map_cols + 2 * LANES + side), F32)],
    )(*arrived)


def quarter_weight(ids, roughness):
    weights = jnp.full(ids.shape, roughness[0])
    for level in range(1, CLASSES):
        weights = jnp.where(ids == float(level), roughness[level], weights)
    return 0.25 * weights


def blend_kernel(roughness, classes, beside, share):
    rows_dev, cols_dev = classes.shape
    left = lax.axis_index("tile") == 0
    for at in range(0, rows_dev, HALO):
        rows = slice(at, at + HALO)
        near = quarter_weight(beside[rows, :].astype(F32), roughness)
        share[rows, 0:LANES] = jnp.where(left, 0.0, near)
        share[rows, LANES + cols_dev :] = jnp.where(left, near, 0.0)
        share[rows, LANES : LANES + cols_dev] = quarter_weight(classes[rows, :].astype(F32), roughness)


def smooth_kernel(roughness, keep, got, inner, out, share, buf_a, buf_b, done, sems):
    rows_dev, cols_dev = out.shape
    window, cut = share.shape
    left = lax.axis_index("tile") == 0
    storm = lax.axis_index("storm")
    lane = lax.broadcasted_iota(jnp.int32, (HALO, cut), 1)
    within = (lane >= jnp.where(left, LANES, 0)) & (lane < jnp.where(left, cut, LANES + cols_dev))
    lines = jnp.maximum(keep[window:, :], got[window:, :]).astype(F32)
    for at, line, inside in (
        (0, 0, storm > 0),
        (window - HALO, HALO, storm < lax.axis_size("storm") - 1),
    ):
        weights = quarter_weight(lines[line : line + HALO], roughness)
        share[at : at + HALO, :] = jnp.where(within, jnp.where(inside, weights, 0.0), 0.0)
    share[HALO : HALO + rows_dev, :] = inner[...]
    pad = HALO
    chunk = 8
    bufs = (buf_a, buf_b)
    for buf in bufs:
        buf[0:pad, :] = jnp.zeros((pad, cut), F32)
        buf[pad + window :, :] = jnp.zeros((pad, cut), F32)
    buf_a[pad : pad + window, :] = jnp.maximum(keep[0:window, :], got[0:window, :]).astype(F32)
    sends = []
    for step in range(PASSES):
        src, dst = bufs[step % 2], bufs[(step + 1) % 2]
        final = step + 1 == PASSES
        for row in range(HALO if final else 0, window - HALO if final else window, chunk):
            at = pad + row
            v = src[at : at + chunk, :]
            around = (
                src[at - 1 : at - 1 + chunk, :]
                + src[at + 1 : at + 1 + chunk, :]
                + pltpu.roll(v, 1, 1)
                + pltpu.roll(v, cut - 1, 1)
            )
            w = share[row : row + chunk, :]
            new = v - 4.0 * w * v + w * around
            if final:
                to = row - HALO
                done[to : to + chunk, :] = new[:, LANES : LANES + cols_dev]
                if (to + chunk) % SEND_ROWS == 0:
                    part = pl.ds(to + chunk - SEND_ROWS, SEND_ROWS)
                    sends.append(pltpu.make_async_copy(done.at[part], out.at[part], sems.at[to // SEND_ROWS]))
                    sends[-1].start()
            else:
                dst[at : at + chunk, :] = jnp.where(w > 0.0, new, 0.0)
    for send in sends:
        send.wait()


FAR_FIRST = ((10, 11), (9, 1), (12, 13), (15, 2), (5, 7), (3, 4), (6, 8), (0, 14))


def routes(storms):
    group = 2 * len(FAR_FIRST)
    if storms % group:
        return [(k, k + storms // 2) for k in range(storms // 2)]
    return [(base + a, base + b) for base in range(0, storms, group) for a, b in FAR_FIRST]


def window_map(patches, patch_coeffs, row_offset, col_offset, live_counts, class_map, roughness):
    storms = lax.axis_size("storm")
    rows_dev, cols_dev = class_map.shape
    tiles = lax.axis_size("tile")
    map_cols = cols_dev * tiles
    smem = pl.BlockSpec(memory_space=pltpu.SMEM)
    vmem = pl.BlockSpec(memory_space=pltpu.VMEM)
    window = rows_dev + 2 * HALO
    cut = cols_dev + 2 * LANES
    t = lax.axis_index("tile")
    swap = [(0, 1), (1, 0)]
    hops = routes(storms)

    own, give = make_slabs(patches, patch_coeffs, row_offset, col_offset, live_counts, class_map, hops)
    both = jnp.stack([own, lax.ppermute(give, "tile", swap)], axis=1)
    both, ids = lax.optimization_barrier((both, class_map))
    items = []
    for item, (a, b) in enumerate(hops):
        pairs = [(2 * i + j, 2 * (i ^ k) + j) for i in range(storms) for j, k in enumerate((a, b))]
        items.append(lax.ppermute(both[item], ("storm", "tile"), pairs))

    edge = lax.dynamic_slice_in_dim(ids, jnp.where(t == 0, cols_dev - LANES, 0), LANES, 1).astype(BF16)
    beside = lax.ppermute(edge, "tile", swap)
    share = pl.pallas_call(
        blend_kernel,
        name="blend",
        compiler_params=SMALL,
        out_shape=jax.ShapeDtypeStruct((rows_dev, cut), F32),
        in_specs=[smem, vmem, vmem],
        out_specs=vmem,
    )(roughness, class_map, beside)

    *items, share = lax.optimization_barrier((*items, share))
    keep, give = stamp(items, hops, rows_dev, cols_dev, map_cols)
    got = lax.ppermute(give, "tile", swap)
    return pl.pallas_call(
        smooth_kernel,
        name="smooth",
        compiler_params=SMALL,
        out_shape=jax.ShapeDtypeStruct((rows_dev, cols_dev), F32),
        in_specs=[smem, vmem, vmem, vmem],
        out_specs=pl.BlockSpec(memory_space=pl.ANY),
        scratch_shapes=[
            pltpu.VMEM((window, cut), F32),
            pltpu.VMEM((window + 2 * HALO, cut), F32),
            pltpu.VMEM((window + 2 * HALO, cut), F32),
            pltpu.VMEM((rows_dev, cols_dev), F32),
            pltpu.SemaphoreType.DMA((rows_dev // SEND_ROWS,)),
        ],
    )(roughness, keep, got, share)


def solution(mesh):
    return jax.shard_map(
        window_map,
        mesh=mesh,
        in_specs=(
            P(("grp", "storm", "tile"), None, None, None),
            P(("grp", "storm", "tile"), None),
            P(("grp", "storm", "tile")),
            P(("grp", "storm", "tile")),
            P(("grp", "storm", "tile")),
            P(("grp", "storm"), "tile"),
            P(),
        ),
        out_specs=P(("grp", "storm"), "tile"),
        check_vma=False,
    )
```

```python
import functools

import jax
import jax.numpy as jnp
from jax import lax
from jax.experimental import pallas as pl
from jax.experimental.pallas import tpu as pltpu
from jax.sharding import PartitionSpec as P


STEPS = 6
CLASSES = 16
PASSES = 4
HALO = 8
LANES = 128
SMALL = pltpu.CompilerParams(vmem_limit_bytes=16 * 1024 * 1024)
F32 = jnp.float32
BF16 = jnp.bfloat16


def spread(side):
    column = lax.broadcasted_iota(jnp.int32, (side, side), 0)
    place = lax.broadcasted_iota(jnp.int32, (side, side), 1)
    parts = side // LANES
    return jnp.where(column == parts * lax.rem(place, LANES) + lax.div(place, LANES), 1.0, 0.0).astype(BF16)


def gather_turned(side, turn):
    place = lax.broadcasted_iota(jnp.int32, (side, side), 0)
    column = lax.broadcasted_iota(jnp.int32, (side, side), 1)
    parts = side // LANES
    moved = parts * lax.rem(place, LANES) + lax.div(place, LANES) + turn
    moved = jnp.where(moved >= side, moved - side, moved)
    return jnp.where(column == moved, 1.0, 0.0).astype(BF16)


def select_columns(x, one_hot):
    total = None
    for term in range(3):
        piece = x.astype(BF16)
        product = jnp.dot(piece, one_hot, preferred_element_type=F32)
        total = product if total is None else total + product
        if term < 2:
            x = x - piece.astype(F32)
    return total


def advance_into(source, drag, turn, bufs, gust, lead, side):
    tiles = side // HALO + 1
    count = side // LANES
    lane = lax.broadcasted_iota(jnp.int32, (HALO, LANES), 1)
    row = lax.broadcasted_iota(jnp.int32, (HALO, LANES), 0)
    first, last = lane == 0, lane == LANES - 1
    parts = [slice(c * LANES, (c + 1) * LANES) for c in range(count)]

    def sides(v):
        before = [jnp.where(first, 0.0, pltpu.roll(v[-1], 1, 1))] + v[:-1]
        after = v[1:] + [jnp.where(last, 0.0, pltpu.roll(v[0], LANES - 1, 1))]
        return [x + y for x, y in zip(before, after)]

    def put(buf, field, k, c, v):
        if k + (HALO - 1) * tiles >= side:
            v = jnp.where(row == HALO - 1, 0.0, v)
        buf[field, k + 1, :, parts[c]] = v
        if k == tiles - 1:
            buf[field, 0, :, parts[c]] = jnp.where(row == 0, 0.0, pltpu.roll(v, 1, 0))
        if k == 0:
            buf[field, tiles + 1, :, parts[c]] = jnp.where(row == HALO - 1, 0.0, pltpu.roll(v, HALO - 1, 0))

    for field in range(2):
        for k in range(tiles):
            for c in range(count):
                put(bufs[0], field, k, c, source[field, c, pl.ds(k, HALO, stride=tiles), :])
    turn = 5.0 * turn
    for step in range(STEPS):
        src, dst = bufs[step % 2], bufs[(step + 1) % 2]
        scale = 0.2**step
        pull = drag * (5.0 * scale)
        for k in range(tiles):
            e = [src[0, k + 1, :, p] for p in parts]
            n = [src[1, k + 1, :, p] for p in parts]
            side_e, side_n = sides(e), sides(n)
            for c, p in enumerate(parts):
                power = e[c] * e[c] + n[c] * n[c] + 0.25 / scale**2
                keep = 1.0 - pull * (power * lax.rsqrt(power))
                around_e = (src[0, k, :, p] + src[0, k + 2, :, p]) + side_e[c]
                around_n = (src[1, k, :, p] + src[1, k + 2, :, p]) + side_n[c]
                e_new = around_e + e[c] * keep + turn * n[c]
                n_new = around_n + n[c] * keep - turn * e[c]
                if step + 1 < STEPS:
                    put(dst, 0, k, c, e_new)
                    put(dst, 1, k, c, n_new)
                else:
                    power = e_new * e_new + n_new * n_new + 0.25 / (0.2 * scale) ** 2
                    v = (0.2 * scale) * (power * lax.rsqrt(power))
                    if k + (HALO - 1) * tiles >= side:
                        v = jnp.where(row == HALO - 1, 0.0, v)
                    gust[c, pl.ds(lead + k, HALO, stride=tiles), :] = v


def slabs_kernel(
    hops,
    rows_dev,
    counts,
    row_hbm,
    col_hbm,
    coeffs_hbm,
    classes,
    patches,
    own,
    give,
    row_off,
    col_off,
    coeffs,
    loaded,
    buf_a,
    buf_b,
    gusts,
    edges,
    sems,
    small_sems,
):
    smalls = [
        pltpu.make_async_copy(source, target, small_sems.at[i])
        for i, (source, target) in enumerate(
            (
                (row_hbm, row_off),
                (col_hbm, col_off),
                (coeffs_hbm, coeffs),
                (classes.at[pl.ds(0, HALO), :], edges.at[0]),
                (classes.at[pl.ds(rows_dev - HALO, HALO), :], edges.at[1]),
            )
        )
    ]
    for copy in smalls:
        copy.start()
    side = patches.shape[3]
    parts = side // LANES
    window = rows_dev + 2 * HALO
    half = len(hops)
    storm, tile = lax.axis_index("storm"), lax.axis_index("tile")

    def fetch(slot, field):
        return [
            pltpu.make_async_copy(
                patches.at[slot, field, :, pl.ds(c * LANES, LANES)],
                loaded.at[slot, field, c, pl.ds(0, side), :],
                sems.at[slot, field, c],
            )
            for c in range(parts)
        ]

    for slot in range(2):

        @pl.when(counts[0] > slot)
        def _():
            for field in range(2):
                for copy in fetch(slot, field):
                    copy.start()

    row = lax.broadcasted_iota(jnp.int32, (HALO, side), 0)
    lane = lax.broadcasted_iota(jnp.int32, (HALO, side), 1)
    for slot in range(2):
        loaded[slot, :, :, side:, :] = jnp.zeros((2, parts, loaded.shape[3] - side, LANES), F32)
        gusts[slot, :, 0:window, :] = jnp.zeros((parts, window, LANES), F32)
        gusts[slot, :, window + side :, :] = jnp.zeros((parts, window + HALO, LANES), F32)

    def rows(slot, block, skip, count):
        base = lax.div(row_off[slot], HALO) * HALO
        at = jnp.clip(block * rows_dev - HALO - base, -window, side + HALO) + window + skip
        at = pl.ds(pl.multiple_of(at, HALO), count)
        return jnp.concatenate([gusts[slot, c, at, :] for c in range(parts)], axis=1)

    def build(out, item, block):
        main = jnp.where(block < half, 0, 1)
        other = 1 - main
        head = rows(jnp.where(block == half, other, main), block, 0, HALO)
        body = rows(main, block, HALO, rows_dev)
        tail = rows(jnp.where(block == half - 1, other, main), block, HALO + rows_dev, HALO)
        for line, slot in ((0, main), (2, other)):
            major = lax.div(col_off[slot], side)
            minor = col_off[slot] - major * side
            head = jnp.where(row == line, major.astype(F32), head)
            head = jnp.where(row == line + 1, jnp.where(lane >= minor, 1.0, 0.0), head)
        out[item, 0:window, :] = jnp.concatenate([head, body, tail], axis=0).astype(out.dtype)
        lines = jnp.where(block == storm + 1, bottom, jnp.where(block == storm - 1, top, 0.0))
        out[item, window:, :] = lines.astype(out.dtype)

    for copy in smalls:
        copy.wait()
    for slot in range(2):
        live = counts[0] > slot

        @pl.when(live)
        def _():
            gusts[slot, :, window : window + HALO, :] = jnp.zeros((parts, HALO, LANES), F32)
            one_hot = spread(side)
            for field in range(2):
                for copy in fetch(slot, field):
                    copy.wait()
                both = jnp.concatenate([loaded[slot, field, c, 0:side, :] for c in range(parts)], axis=1)
                both = select_columns(both, one_hot)
                for c in range(parts):
                    loaded[slot, field, c, 0:side, :] = both[:, c * LANES : (c + 1) * LANES]
            advance_into(
                loaded.at[slot],
                coeffs[slot, 0],
                coeffs[slot, 1],
                (buf_a, buf_b),
                gusts.at[slot],
                window + lax.rem(row_off[slot], HALO),
                side,
            )
            body = slice(window, window + side + HALO)
            both = jnp.concatenate([gusts[slot, c, body, :] for c in range(parts)], axis=1).astype(BF16)
            both = jnp.dot(both, gather_turned(side, lax.rem(col_off[slot], side)), preferred_element_type=F32)
            for c in range(parts):
                gusts[slot, c, body, :] = both[:, c * LANES : (c + 1) * LANES]

        @pl.when(jnp.logical_not(live))
        def _():
            gusts[slot, :, window : window + side, :] = jnp.zeros((parts, side, LANES), F32)

    def folded(lines):
        lines = lines.astype(F32)
        return jnp.concatenate([lines[:, at : at + side] for at in range(0, lines.shape[1], side)], axis=0)

    top, bottom = folded(edges[0, 0:PASSES, :]), folded(edges[1, HALO - PASSES : HALO, :])
    for item, (a, b) in enumerate(hops):
        build(own, item, storm ^ jnp.where(tile == 0, a, b))
        build(give, item, storm ^ jnp.where(tile == 0, b, a))


def make_slabs(patches, coeffs, row_off, col_off, counts, classes, hops):
    side = patches.shape[3]
    parts = side // LANES
    rows_dev, cols_dev = classes.shape
    window = rows_dev + 2 * HALO
    hbm = pl.BlockSpec(memory_space=pltpu.HBM)
    vmem = pl.BlockSpec(memory_space=pltpu.VMEM)
    result = jax.ShapeDtypeStruct((len(hops), window + PASSES * cols_dev // side, side), BF16)
    return pl.pallas_call(
        functools.partial(slabs_kernel, hops, rows_dev),
        name="slabs",
        out_shape=(result, result),
        compiler_params=SMALL,
        in_specs=[pl.BlockSpec(memory_space=pltpu.SMEM)] + [hbm] * 5,
        out_specs=(vmem, vmem),
        scratch_shapes=[
            pltpu.SMEM(row_off.shape, row_off.dtype),
            pltpu.SMEM(col_off.shape, col_off.dtype),
            pltpu.SMEM(coeffs.shape, coeffs.dtype),
            pltpu.VMEM((2, 2, parts, side + side // HALO + HALO, LANES), F32),
            pltpu.VMEM((2, side // HALO + 3, HALO, side), F32),
            pltpu.VMEM((2, side // HALO + 3, HALO, side), F32),
            pltpu.VMEM((2, parts, side + 2 * window + HALO, LANES), F32),
            pltpu.VMEM((2, HALO, cols_dev), classes.dtype),
            pltpu.SemaphoreType.DMA((2, 2, parts)),
            pltpu.SemaphoreType.DMA((5,)),
        ],
        cost_estimate=pl.CostEstimate(flops=40 * STEPS * patches.size // 2, bytes_accessed=2 * patches.size, transcendentals=0),
    )(counts, *(pltpu.with_memory_space_constraint(x, pltpu.HBM) for x in (row_off, col_off, coeffs, classes, patches)))


def stamp_kernel(cols_dev, window, hops, *refs):
    arrived, (keep, give, strip) = refs[: len(hops)], refs[len(hops) :]
    items = [ref.at[part] for ref in arrived for part in range(ref.shape[0])]
    side = arrived[0].shape[2]
    strip[...] = jnp.zeros_like(strip)
    storm, tile = lax.axis_index("storm"), lax.axis_index("tile")
    storms = lax.axis_size("storm")
    upper_edge = storm == storms // 2 - 1
    lower_edge = storm == storms // 2
    tail_row = window - HALO
    cut = cols_dev + 2 * LANES

    def put(at, rows, value, mask):
        zero = jnp.zeros_like(value)
        col = pl.multiple_of(LANES + at * side, LANES)
        lo = (slice(rows, rows + value.shape[0]), pl.ds(col, side))
        hi = (slice(rows, rows + value.shape[0]), pl.ds(pl.multiple_of(col + side, LANES), side))
        strip[lo] = jnp.maximum(strip[lo], jnp.where(mask, value, zero))
        strip[hi] = jnp.maximum(strip[hi], jnp.where(mask, zero, value))

    count = len(items)

    def column(item, at):
        return items[item][0:16, 0:LANES].astype(F32)[at, 0].astype(jnp.int32)

    columns = [column(item, 0) for item in range(count)]
    for item in range(count):
        slab = items[item][0:window, :].astype(F32)
        head, body, tail = slab[0:HALO], slab[HALO:tail_row], slab[tail_row:]
        head = jnp.where(lower_edge, 0.0, head)
        tail = jnp.where(upper_edge, 0.0, tail)
        mask = slab[1:2, :] > 0.5
        put(columns[item], 0, jnp.concatenate([head, body, tail], axis=0), mask)

    def other(rows):
        columns = [column(item, 2) for item in range(count)]
        for item in range(count):
            mask = items[item][0:HALO, :].astype(F32)[3:4, :] > 0.5
            put(columns[item], rows, items[item][rows : rows + HALO, :].astype(F32), mask)

    pl.when(lower_edge)(lambda: other(0))
    pl.when(upper_edge)(lambda: other(tail_row))

    for item, (a, b) in enumerate(hops):
        source = storm ^ jnp.where(tile == 0, a, b)

        def lines(to):
            for part in range(arrived[item].shape[0]):
                values = arrived[item][part, window:, :].astype(F32)
                for fold in range(cols_dev // side):
                    at = LANES + jnp.where(tile == part, 0, cols_dev) + fold * side
                    at = pl.ds(pl.multiple_of(at, LANES), side)
                    strip[to : to + PASSES, at] = values[fold * PASSES : (fold + 1) * PASSES]

        pl.when(source == storm - 1)(lambda: lines(window + HALO - PASSES))
        pl.when(source == storm + 1)(lambda: lines(window + HALO))

    own = pl.multiple_of(tile * cols_dev, LANES)
    away = pl.multiple_of((1 - tile) * cols_dev, LANES)
    keep[...] = strip[:, pl.ds(own, cut)].astype(keep.dtype)
    give[...] = strip[:, pl.ds(away, cut)].astype(give.dtype)


def stamp(arrived, hops, rows_dev, cols_dev, map_cols):
    side = arrived[0].shape[2]
    window = rows_dev + 2 * HALO
    height = window + 2 * HALO
    cut = cols_dev + 2 * LANES
    vmem = pl.BlockSpec(memory_space=pltpu.VMEM)
    return pl.pallas_call(
        functools.partial(stamp_kernel, cols_dev, window, hops),
        name="stamp",
        compiler_params=SMALL,
        out_shape=(jax.ShapeDtypeStruct((height, cut), BF16), jax.ShapeDtypeStruct((height, cut), BF16)),
        in_specs=[vmem] * len(arrived),
        out_specs=(vmem, vmem),
        scratch_shapes=[pltpu.VMEM((height, map_cols + 2 * LANES + side), F32)],
    )(*arrived)


def quarter_weight(ids, roughness):
    weights = jnp.full(ids.shape, roughness[0])
    for level in range(1, CLASSES):
        weights = jnp.where(ids == float(level), roughness[level], weights)
    return 0.25 * weights


def blend_kernel(roughness, classes, beside, stay, share):
    rows_dev, cols_dev = classes.shape
    left = lax.axis_index("tile") == 0

    def fill(rows, cols, ids, inside):
        weights = quarter_weight(ids, roughness)
        rest = 1.0 - 4.0 * weights
        if inside is not None:
            weights, rest = jnp.where(inside, weights, 0.0), jnp.where(inside, rest, 0.0)
        stay[rows, cols] = rest
        share[rows, cols] = weights

    for at in range(0, rows_dev, HALO):
        rows = slice(at, at + HALO)
        near = beside[rows, :].astype(F32)
        fill(rows, slice(0, LANES), near, jnp.logical_not(left))
        fill(rows, slice(LANES + cols_dev, 2 * LANES + cols_dev), near, left)
        fill(rows, slice(LANES, LANES + cols_dev), classes[rows, :].astype(F32), None)


def smooth_kernel(roughness, keep, got, stay, share, out, halo, buf_a, buf_b, done, sems):
    rows_dev, cols_dev = out.shape
    cut = share.shape[1]
    window = rows_dev + 2 * HALO
    left = lax.axis_index("tile") == 0
    storm = lax.axis_index("storm")
    bufs = (buf_a, buf_b)
    for buf in bufs:
        buf[0:HALO, :] = jnp.zeros((HALO, cut), F32)
        buf[HALO + window :, :] = jnp.zeros((HALO, cut), F32)
    buf_a[HALO : HALO + window, :] = jnp.maximum(keep[0:window, :], got[0:window, :]).astype(F32)
    lane = lax.broadcasted_iota(jnp.int32, (HALO, cut), 1)
    within = (lane >= jnp.where(left, LANES, 0)) & (lane < jnp.where(left, cut, LANES + cols_dev))
    lines = jnp.maximum(keep[window:, :], got[window:, :]).astype(F32)
    for at, inside in ((0, storm > 0), (1, storm < lax.axis_size("storm") - 1)):
        weights = quarter_weight(lines[at * HALO : (at + 1) * HALO], roughness)
        rest = 1.0 - 4.0 * weights
        halo[at, 0] = jnp.where(within, jnp.where(inside, rest, 0.0), 0.0)
        halo[at, 1] = jnp.where(within, jnp.where(inside, weights, 0.0), 0.0)

    def factors(row, count, cols):
        top, end = max(row, HALO), min(row + count, HALO + rows_dev)
        both = [[stay[top - HALO : end - HALO, cols]], [share[top - HALO : end - HALO, cols]]]
        for kind in range(2):
            if row < HALO:
                both[kind].insert(0, halo[0, kind, :, cols])
            if row + count > HALO + rows_dev:
                both[kind].append(halo[1, kind, :, cols])
        return [jnp.concatenate(x, axis=0) if len(x) > 1 else x[0] for x in both]

    sends = []
    tiles = [slice(c, c + LANES) for c in range(0, cut, LANES)]
    for step in range(PASSES):
        src, dst = bufs[step % 2], bufs[(step + 1) % 2]
        final = step + 1 == PASSES
        first_row, last_row = (HALO, HALO + rows_dev) if final else (0, window)
        chunk = (last_row - first_row) // 2
        one = lax.broadcasted_iota(jnp.int32, (chunk, LANES), 1)
        for row in range(first_row, last_row, chunk):
            at = HALO + row
            middle, right, back = [], [], []

            def load(c):
                middle.append(src[at : at + chunk, tiles[c]])
                right.append(pltpu.roll(middle[c], 1, 1))
                back.append(pltpu.roll(middle[c], LANES - 1, 1))

            load(0)
            for c, cols in enumerate(tiles):
                if c + 1 < len(tiles):
                    load(c + 1)
                if final and c in (0, len(tiles) - 1):
                    continue
                before = jnp.where(one == 0, right[c - 1], right[c]) if c else right[c]
                after = jnp.where(one == LANES - 1, back[c + 1], back[c]) if c + 1 < len(tiles) else back[c]
                around = (src[at - 1 : at - 1 + chunk, cols] + src[at + 1 : at + 1 + chunk, cols]) + (before + after)
                rest, quarter = factors(row, chunk, cols)
                new = rest * middle[c] + quarter * around
                if final:
                    done[row - HALO : row - HALO + chunk, tiles[c - 1]] = new
                else:
                    dst[at : at + chunk, cols] = new
            if final:
                part = pl.ds(row - HALO, chunk)
                sends.append(pltpu.make_async_copy(done.at[part], out.at[part], sems.at[len(sends)]))
                sends[-1].start()
    for send in sends:
        send.wait()


FAR_FIRST = ((10, 8), (9, 1), (14, 11), (13, 2), (5, 7), (3, 4), (6, 15), (0, 12))


def routes(storms):
    group = 2 * len(FAR_FIRST)
    if storms % group:
        return [(k, k + storms // 2) for k in range(storms // 2)]
    return [(base + a, base + b) for base in range(0, storms, group) for a, b in FAR_FIRST]


def window_map(patches, patch_coeffs, row_offset, col_offset, live_counts, class_map, roughness):
    storms = lax.axis_size("storm")
    rows_dev, cols_dev = class_map.shape
    tiles = lax.axis_size("tile")
    map_cols = cols_dev * tiles
    smem = pl.BlockSpec(memory_space=pltpu.SMEM)
    vmem = pl.BlockSpec(memory_space=pltpu.VMEM)
    window = rows_dev + 2 * HALO
    cut = cols_dev + 2 * LANES
    t = lax.axis_index("tile")
    swap = [(0, 1), (1, 0)]
    hops = routes(storms)

    own, give = make_slabs(patches, patch_coeffs, row_offset, col_offset, live_counts, class_map, hops)
    cut_at = len(hops) // 2
    both = []
    for part in (slice(0, cut_at), slice(cut_at, len(hops))):
        theirs = lax.ppermute(give[part], "tile", swap)
        both.append(jnp.stack([own[part], theirs], axis=1))
    both[0], ids = lax.optimization_barrier((both[0], class_map))
    items = []
    for item, (a, b) in enumerate(hops):
        pairs = [(2 * i + j, 2 * (i ^ k) + j) for i in range(storms) for j, k in enumerate((a, b))]
        items.append(lax.ppermute(both[item // cut_at][item % cut_at], ("storm", "tile"), pairs))

    edge = lax.dynamic_slice_in_dim(ids, jnp.where(t == 0, cols_dev - LANES, 0), LANES, 1).astype(BF16)
    beside = lax.ppermute(edge, "tile", swap)
    factors = jax.ShapeDtypeStruct((rows_dev, cut), F32)
    stay, share = pl.pallas_call(
        blend_kernel,
        name="blend",
        compiler_params=SMALL,
        out_shape=(factors, factors),
        in_specs=[smem, vmem, vmem],
        out_specs=(vmem, vmem),
    )(roughness, class_map, beside)

    *items, stay, share = lax.optimization_barrier((*items, stay, share))
    keep, give = stamp(items, hops, rows_dev, cols_dev, map_cols)
    got = lax.ppermute(give, "tile", swap)
    return pl.pallas_call(
        smooth_kernel,
        name="smooth",
        compiler_params=SMALL,
        out_shape=jax.ShapeDtypeStruct((rows_dev, cols_dev), F32),
        in_specs=[smem, vmem, vmem, vmem, vmem],
        out_specs=pl.BlockSpec(memory_space=pl.ANY),
        scratch_shapes=[
            pltpu.VMEM((2, 2, HALO, cut), F32),
            pltpu.VMEM((window + 2 * HALO, cut), F32),
            pltpu.VMEM((window + 2 * HALO, cut), F32),
            pltpu.VMEM((rows_dev, cols_dev), F32),
            pltpu.SemaphoreType.DMA((2,)),
        ],
    )(roughness, keep, got, stay, share)


def solution(mesh):
    return jax.shard_map(
        window_map,
        mesh=mesh,
        in_specs=(
            P(("grp", "storm", "tile"), None, None, None),
            P(("grp", "storm", "tile"), None),
            P(("grp", "storm", "tile")),
            P(("grp", "storm", "tile")),
            P(("grp", "storm", "tile")),
            P(("grp", "storm"), "tile"),
            P(),
        ),
        out_specs=P(("grp", "storm"), "tile"),
        check_vma=False,
    )
```

```python
import functools

import jax
import jax.numpy as jnp
from jax import lax
from jax.experimental import pallas as pl
from jax.experimental.pallas import tpu as pltpu
from jax.sharding import PartitionSpec as P


STEPS = 6
CLASSES = 16
PASSES = 4
HALO = 8
LANES = 128
SMALL = pltpu.CompilerParams(vmem_limit_bytes=16 * 1024 * 1024)
F32 = jnp.float32
BF16 = jnp.bfloat16


def one_hot(rows):
    side = rows.shape[1]
    place = lax.broadcasted_iota(jnp.int32, (side, side), 0)
    return jnp.where(place == rows, 1.0, 0.0).astype(BF16)


def spread(side):
    place = lax.broadcasted_iota(jnp.int32, (1, side), 1)
    return one_hot(side // LANES * lax.rem(place, LANES) + lax.div(place, LANES))


def gather_turned(side, turn):
    parts = side // LANES
    column = lax.broadcasted_iota(jnp.int32, (1, side), 1) - turn
    column = jnp.where(column < 0, column + side, column)
    return one_hot(lax.rem(column, parts) * LANES + lax.div(column, parts))


def select_columns(x, places):
    total = None
    for term in range(3):
        piece = x.astype(BF16)
        product = jnp.dot(piece, places, preferred_element_type=F32)
        total = product if total is None else total + product
        if term < 2:
            x = x - piece.astype(F32)
    return total


def advance_into(source, drag, turn, bufs, gust, lead, side):
    tiles = side // HALO + 1
    count = side // LANES
    lane = lax.broadcasted_iota(jnp.int32, (HALO, LANES), 1)
    row = lax.broadcasted_iota(jnp.int32, (HALO, LANES), 0)
    first, last = lane == 0, lane == LANES - 1
    parts = [slice(c * LANES, (c + 1) * LANES) for c in range(count)]

    def sides(v):
        before = [jnp.where(first, 0.0, pltpu.roll(v[-1], 1, 1))] + v[:-1]
        after = v[1:] + [jnp.where(last, 0.0, pltpu.roll(v[0], LANES - 1, 1))]
        return [x + y for x, y in zip(before, after)]

    def put(buf, field, k, c, v):
        if k + (HALO - 1) * tiles >= side:
            v = jnp.where(row == HALO - 1, 0.0, v)
        buf[field, k + 1, :, parts[c]] = v
        if k == tiles - 1:
            buf[field, 0, :, parts[c]] = jnp.where(row == 0, 0.0, pltpu.roll(v, 1, 0))
        if k == 0:
            buf[field, tiles + 1, :, parts[c]] = jnp.where(row == HALO - 1, 0.0, pltpu.roll(v, HALO - 1, 0))

    for field in range(2):
        for k in range(tiles):
            for c in range(count):
                put(bufs[0], field, k, c, source[field, c, pl.ds(k, HALO, stride=tiles), :])
    turn = 5.0 * turn
    for step in range(STEPS):
        src, dst = bufs[step % 2], bufs[(step + 1) % 2]
        scale = 0.2**step
        pull = drag * (5.0 * scale)
        for k in range(tiles):
            e = [src[0, k + 1, :, p] for p in parts]
            n = [src[1, k + 1, :, p] for p in parts]
            side_e, side_n = sides(e), sides(n)
            for c, p in enumerate(parts):
                power = e[c] * e[c] + n[c] * n[c] + 0.25 / scale**2
                keep = 1.0 - pull * (power * lax.rsqrt(power))
                around_e = (src[0, k, :, p] + src[0, k + 2, :, p]) + side_e[c]
                around_n = (src[1, k, :, p] + src[1, k + 2, :, p]) + side_n[c]
                e_new = around_e + e[c] * keep + turn * n[c]
                n_new = around_n + n[c] * keep - turn * e[c]
                if step + 1 < STEPS:
                    put(dst, 0, k, c, e_new)
                    put(dst, 1, k, c, n_new)
                else:
                    power = e_new * e_new + n_new * n_new + 0.25 / (0.2 * scale) ** 2
                    v = (0.2 * scale) * (power * lax.rsqrt(power))
                    if k + (HALO - 1) * tiles >= side:
                        v = jnp.where(row == HALO - 1, 0.0, v)
                    gust[c, pl.ds(lead + k, HALO, stride=tiles), :] = v


def slabs_kernel(
    hops,
    rows_dev,
    counts,
    row_hbm,
    col_hbm,
    coeffs_hbm,
    classes,
    patches,
    own,
    give,
    row_off,
    col_off,
    coeffs,
    loaded,
    buf_a,
    buf_b,
    gusts,
    edges,
    hot,
    sems,
    small_sems,
):
    smalls = [
        pltpu.make_async_copy(source, target, small_sems.at[i])
        for i, (source, target) in enumerate(
            (
                (row_hbm, row_off),
                (col_hbm, col_off),
                (coeffs_hbm, coeffs),
                (classes.at[pl.ds(0, HALO), :], edges.at[0]),
                (classes.at[pl.ds(rows_dev - HALO, HALO), :], edges.at[1]),
            )
        )
    ]
    for copy in smalls:
        copy.start()
    side = patches.shape[3]
    parts = side // LANES
    window = rows_dev + 2 * HALO
    half = len(hops)
    storm, tile = lax.axis_index("storm"), lax.axis_index("tile")

    def fetch(slot, field):
        return [
            pltpu.make_async_copy(
                patches.at[slot, field, :, pl.ds(c * LANES, LANES)],
                loaded.at[slot, field, c, pl.ds(0, side), :],
                sems.at[slot, field, c],
            )
            for c in range(parts)
        ]

    for slot in range(2):

        @pl.when(counts[0] > slot)
        def _():
            for field in range(2):
                for copy in fetch(slot, field):
                    copy.start()

    row = lax.broadcasted_iota(jnp.int32, (HALO, side), 0)
    lane = lax.broadcasted_iota(jnp.int32, (HALO, side), 1)
    for slot in range(2):
        loaded[slot, :, :, side:, :] = jnp.zeros((2, parts, loaded.shape[3] - side, LANES), F32)
        gusts[slot, :, 0:window, :] = jnp.zeros((parts, window, LANES), F32)
        gusts[slot, :, window + side :, :] = jnp.zeros((parts, window + HALO, LANES), F32)

    def rows(slot, block, skip, count):
        base = lax.div(row_off[slot], HALO) * HALO
        at = jnp.clip(block * rows_dev - HALO - base, -window, side + HALO) + window + skip
        at = pl.ds(pl.multiple_of(at, HALO), count)
        return jnp.concatenate([gusts[slot, c, at, :] for c in range(parts)], axis=1)

    def build(out, item, block):
        main = jnp.where(block < half, 0, 1)
        other = 1 - main
        head = rows(jnp.where(block == half, other, main), block, 0, HALO)
        body = rows(main, block, HALO, rows_dev)
        tail = rows(jnp.where(block == half - 1, other, main), block, HALO + rows_dev, HALO)
        for line, slot in ((0, main), (2, other)):
            major = lax.div(col_off[slot], side)
            minor = col_off[slot] - major * side
            head = jnp.where(row == line, major.astype(F32), head)
            head = jnp.where(row == line + 1, jnp.where(lane >= minor, 1.0, 0.0), head)
        out[item, 0:window, :] = jnp.concatenate([head, body, tail], axis=0).astype(out.dtype)
        lines = jnp.where(block == storm + 1, bottom, jnp.where(block == storm - 1, top, 0.0))
        out[item, window:, :] = lines.astype(out.dtype)

    hot[2] = spread(side)
    for copy in smalls:
        copy.wait()
    for slot in range(2):
        hot[slot] = gather_turned(side, lax.rem(col_off[slot], side))
    for slot in range(2):
        live = counts[0] > slot

        @pl.when(live)
        def _():
            gusts[slot, :, window : window + HALO, :] = jnp.zeros((parts, HALO, LANES), F32)
            for field in range(2):
                for copy in fetch(slot, field):
                    copy.wait()
                both = jnp.concatenate([loaded[slot, field, c, 0:side, :] for c in range(parts)], axis=1)
                both = select_columns(both, hot[2])
                for c in range(parts):
                    loaded[slot, field, c, 0:side, :] = both[:, c * LANES : (c + 1) * LANES]
            advance_into(
                loaded.at[slot],
                coeffs[slot, 0],
                coeffs[slot, 1],
                (buf_a, buf_b),
                gusts.at[slot],
                window + lax.rem(row_off[slot], HALO),
                side,
            )
            body = slice(window, window + side + HALO)
            both = jnp.concatenate([gusts[slot, c, body, :] for c in range(parts)], axis=1).astype(BF16)
            both = jnp.dot(both, hot[slot], preferred_element_type=F32)
            for c in range(parts):
                gusts[slot, c, body, :] = both[:, c * LANES : (c + 1) * LANES]

        @pl.when(jnp.logical_not(live))
        def _():
            gusts[slot, :, window : window + side, :] = jnp.zeros((parts, side, LANES), F32)

    def folded(lines):
        lines = lines.astype(F32)
        return jnp.concatenate([lines[:, at : at + side] for at in range(0, lines.shape[1], side)], axis=0)

    top, bottom = folded(edges[0, 0:PASSES, :]), folded(edges[1, HALO - PASSES : HALO, :])
    for item, (a, b) in enumerate(hops):
        build(own, item, storm ^ jnp.where(tile == 0, a, b))
        build(give, item, storm ^ jnp.where(tile == 0, b, a))


def make_slabs(patches, coeffs, row_off, col_off, counts, classes, hops):
    side = patches.shape[3]
    parts = side // LANES
    rows_dev, cols_dev = classes.shape
    window = rows_dev + 2 * HALO
    hbm = pl.BlockSpec(memory_space=pltpu.HBM)
    vmem = pl.BlockSpec(memory_space=pltpu.VMEM)
    result = jax.ShapeDtypeStruct((len(hops), window + PASSES * cols_dev // side, side), BF16)
    return pl.pallas_call(
        functools.partial(slabs_kernel, hops, rows_dev),
        name="slabs",
        out_shape=(result, result),
        compiler_params=SMALL,
        in_specs=[pl.BlockSpec(memory_space=pltpu.SMEM)] + [hbm] * 5,
        out_specs=(vmem, vmem),
        scratch_shapes=[
            pltpu.SMEM(row_off.shape, row_off.dtype),
            pltpu.SMEM(col_off.shape, col_off.dtype),
            pltpu.SMEM(coeffs.shape, coeffs.dtype),
            pltpu.VMEM((2, 2, parts, side + side // HALO + HALO, LANES), F32),
            pltpu.VMEM((2, side // HALO + 3, HALO, side), F32),
            pltpu.VMEM((2, side // HALO + 3, HALO, side), F32),
            pltpu.VMEM((2, parts, side + 2 * window + HALO, LANES), F32),
            pltpu.VMEM((2, HALO, cols_dev), classes.dtype),
            pltpu.VMEM((3, side, side), BF16),
            pltpu.SemaphoreType.DMA((2, 2, parts)),
            pltpu.SemaphoreType.DMA((5,)),
        ],
        cost_estimate=pl.CostEstimate(flops=40 * STEPS * patches.size // 2, bytes_accessed=2 * patches.size, transcendentals=0),
    )(counts, *(pltpu.with_memory_space_constraint(x, pltpu.HBM) for x in (row_off, col_off, coeffs, classes, patches)))


def stamp_kernel(cols_dev, window, hops, *refs):
    arrived, (keep, give, strip) = refs[: len(hops)], refs[len(hops) :]
    items = [ref.at[part] for ref in arrived for part in range(ref.shape[0])]
    side = arrived[0].shape[2]
    strip[...] = jnp.zeros_like(strip)
    storm, tile = lax.axis_index("storm"), lax.axis_index("tile")
    storms = lax.axis_size("storm")
    upper_edge = storm == storms // 2 - 1
    lower_edge = storm == storms // 2
    tail_row = window - HALO
    cut = cols_dev + 2 * LANES

    def put(at, rows, value, mask):
        zero = jnp.zeros_like(value)
        col = pl.multiple_of(LANES + at * side, LANES)
        lo = (slice(rows, rows + value.shape[0]), pl.ds(col, side))
        hi = (slice(rows, rows + value.shape[0]), pl.ds(pl.multiple_of(col + side, LANES), side))
        strip[lo] = jnp.maximum(strip[lo], jnp.where(mask, value, zero))
        strip[hi] = jnp.maximum(strip[hi], jnp.where(mask, zero, value))

    count = len(items)

    def column(item, at):
        return items[item][0:16, 0:LANES].astype(F32)[at, 0].astype(jnp.int32)

    columns = [column(item, 0) for item in range(count)]
    for item in range(count):
        slab = items[item][0:window, :].astype(F32)
        head, body, tail = slab[0:HALO], slab[HALO:tail_row], slab[tail_row:]
        head = jnp.where(lower_edge, 0.0, head)
        tail = jnp.where(upper_edge, 0.0, tail)
        mask = slab[1:2, :] > 0.5
        put(columns[item], 0, jnp.concatenate([head, body, tail], axis=0), mask)

    def other(rows):
        columns = [column(item, 2) for item in range(count)]
        for item in range(count):
            mask = items[item][0:HALO, :].astype(F32)[3:4, :] > 0.5
            put(columns[item], rows, items[item][rows : rows + HALO, :].astype(F32), mask)

    pl.when(lower_edge)(lambda: other(0))
    pl.when(upper_edge)(lambda: other(tail_row))

    for item, (a, b) in enumerate(hops):
        source = storm ^ jnp.where(tile == 0, a, b)

        def lines(to):
            for part in range(arrived[item].shape[0]):
                values = arrived[item][part, window:, :].astype(F32)
                for fold in range(cols_dev // side):
                    at = LANES + jnp.where(tile == part, 0, cols_dev) + fold * side
                    at = pl.ds(pl.multiple_of(at, LANES), side)
                    strip[to : to + PASSES, at] = values[fold * PASSES : (fold + 1) * PASSES]

        pl.when(source == storm - 1)(lambda: lines(window + HALO - PASSES))
        pl.when(source == storm + 1)(lambda: lines(window + HALO))

    own = pl.multiple_of(tile * cols_dev, LANES)
    away = pl.multiple_of((1 - tile) * cols_dev, LANES)
    keep[...] = strip[:, pl.ds(own, cut)].astype(keep.dtype)
    give[...] = strip[:, pl.ds(away, cut)].astype(give.dtype)


def stamp(arrived, hops, rows_dev, cols_dev, map_cols):
    side = arrived[0].shape[2]
    window = rows_dev + 2 * HALO
    height = window + 2 * HALO
    cut = cols_dev + 2 * LANES
    vmem = pl.BlockSpec(memory_space=pltpu.VMEM)
    return pl.pallas_call(
        functools.partial(stamp_kernel, cols_dev, window, hops),
        name="stamp",
        compiler_params=SMALL,
        out_shape=(jax.ShapeDtypeStruct((height, cut), BF16), jax.ShapeDtypeStruct((height, cut), BF16)),
        in_specs=[vmem] * len(arrived),
        out_specs=(vmem, vmem),
        scratch_shapes=[pltpu.VMEM((height, map_cols + 2 * LANES + side), F32)],
    )(*arrived)


def quarter_weight(ids, roughness):
    weights = jnp.full(ids.shape, roughness[0])
    for level in range(1, CLASSES):
        weights = jnp.where(ids == float(level), roughness[level], weights)
    return 0.25 * weights


def blend_kernel(roughness, classes, beside, stay, share):
    rows_dev, cols_dev = classes.shape
    left = lax.axis_index("tile") == 0

    def fill(rows, cols, ids, inside):
        weights = quarter_weight(ids, roughness)
        rest = 1.0 - 4.0 * weights
        if inside is not None:
            weights, rest = jnp.where(inside, weights, 0.0), jnp.where(inside, rest, 0.0)
        stay[rows, cols] = rest
        share[rows, cols] = weights

    for at in range(0, rows_dev, HALO):
        rows = slice(at, at + HALO)
        near = beside[rows, :].astype(F32)
        fill(rows, slice(0, LANES), near, jnp.logical_not(left))
        fill(rows, slice(LANES + cols_dev, 2 * LANES + cols_dev), near, left)
        fill(rows, slice(LANES, LANES + cols_dev), classes[rows, :].astype(F32), None)


def smooth_kernel(roughness, keep, got, stay, share, out, halo, buf_a, buf_b, done, sems):
    rows_dev, cols_dev = out.shape
    cut = share.shape[1]
    window = rows_dev + 2 * HALO
    left = lax.axis_index("tile") == 0
    storm = lax.axis_index("storm")
    bufs = (buf_a, buf_b)
    for buf in bufs:
        buf[0:HALO, :] = jnp.zeros((HALO, cut), F32)
        buf[HALO + window :, :] = jnp.zeros((HALO, cut), F32)
    buf_a[HALO : HALO + window, :] = jnp.maximum(keep[0:window, :], got[0:window, :]).astype(F32)
    lane = lax.broadcasted_iota(jnp.int32, (HALO, cut), 1)
    within = (lane >= jnp.where(left, LANES, 0)) & (lane < jnp.where(left, cut, LANES + cols_dev))
    lines = jnp.maximum(keep[window:, :], got[window:, :]).astype(F32)
    for at, inside in ((0, storm > 0), (1, storm < lax.axis_size("storm") - 1)):
        weights = quarter_weight(lines[at * HALO : (at + 1) * HALO], roughness)
        rest = 1.0 - 4.0 * weights
        halo[at, 0] = jnp.where(within, jnp.where(inside, rest, 0.0), 0.0)
        halo[at, 1] = jnp.where(within, jnp.where(inside, weights, 0.0), 0.0)

    def factors(row, count, cols):
        top, end = max(row, HALO), min(row + count, HALO + rows_dev)
        both = [[stay[top - HALO : end - HALO, cols]], [share[top - HALO : end - HALO, cols]]]
        for kind in range(2):
            if row < HALO:
                both[kind].insert(0, halo[0, kind, :, cols])
            if row + count > HALO + rows_dev:
                both[kind].append(halo[1, kind, :, cols])
        return [jnp.concatenate(x, axis=0) if len(x) > 1 else x[0] for x in both]

    sends = []
    tiles = [slice(c, c + LANES) for c in range(0, cut, LANES)]
    for step in range(PASSES):
        src, dst = bufs[step % 2], bufs[(step + 1) % 2]
        final = step + 1 == PASSES
        first_row, last_row = (HALO, HALO + rows_dev) if final else (0, window)
        chunk = (last_row - first_row) // 2
        one = lax.broadcasted_iota(jnp.int32, (chunk, LANES), 1)
        for row in range(first_row, last_row, chunk):
            at = HALO + row
            middle, right, back = [], [], []

            def load(c):
                middle.append(src[at : at + chunk, tiles[c]])
                right.append(pltpu.roll(middle[c], 1, 1))
                back.append(pltpu.roll(middle[c], LANES - 1, 1))

            load(0)
            for c, cols in enumerate(tiles):
                if c + 1 < len(tiles):
                    load(c + 1)
                if final and c in (0, len(tiles) - 1):
                    continue
                before = jnp.where(one == 0, right[c - 1], right[c]) if c else right[c]
                after = jnp.where(one == LANES - 1, back[c + 1], back[c]) if c + 1 < len(tiles) else back[c]
                around = (src[at - 1 : at - 1 + chunk, cols] + src[at + 1 : at + 1 + chunk, cols]) + (before + after)
                rest, quarter = factors(row, chunk, cols)
                new = rest * middle[c] + quarter * around
                if final:
                    done[row - HALO : row - HALO + chunk, tiles[c - 1]] = new
                else:
                    dst[at : at + chunk, cols] = new
            if final:
                part = pl.ds(row - HALO, chunk)
                sends.append(pltpu.make_async_copy(done.at[part], out.at[part], sems.at[len(sends)]))
                sends[-1].start()
    for send in sends:
        send.wait()


FAR_FIRST = ((10, 8), (9, 1), (14, 11), (13, 2), (5, 7), (3, 4), (6, 15), (0, 12))


def routes(storms):
    group = 2 * len(FAR_FIRST)
    if storms % group:
        return [(k, k + storms // 2) for k in range(storms // 2)]
    return [(base + a, base + b) for base in range(0, storms, group) for a, b in FAR_FIRST]


def window_map(patches, patch_coeffs, row_offset, col_offset, live_counts, class_map, roughness):
    storms = lax.axis_size("storm")
    rows_dev, cols_dev = class_map.shape
    tiles = lax.axis_size("tile")
    map_cols = cols_dev * tiles
    smem = pl.BlockSpec(memory_space=pltpu.SMEM)
    vmem = pl.BlockSpec(memory_space=pltpu.VMEM)
    window = rows_dev + 2 * HALO
    cut = cols_dev + 2 * LANES
    t = lax.axis_index("tile")
    swap = [(0, 1), (1, 0)]
    hops = routes(storms)

    own, give = make_slabs(patches, patch_coeffs, row_offset, col_offset, live_counts, class_map, hops)
    cut_at = max(1, len(hops) // 4)
    both = []
    for part in (slice(0, cut_at), slice(cut_at, len(hops))):
        theirs = lax.ppermute(give[part], "tile", swap)
        both.append(jnp.stack([own[part], theirs], axis=1))
    both[0], ids = lax.optimization_barrier((both[0], class_map))
    items = []
    for item, (a, b) in enumerate(hops):
        pairs = [(2 * i + j, 2 * (i ^ k) + j) for i in range(storms) for j, k in enumerate((a, b))]
        ready = both[0][item] if item < cut_at else both[1][item - cut_at]
        items.append(lax.ppermute(ready, ("storm", "tile"), pairs))

    edge = lax.dynamic_slice_in_dim(ids, jnp.where(t == 0, cols_dev - LANES, 0), LANES, 1).astype(BF16)
    beside = lax.ppermute(edge, "tile", swap)
    factors = jax.ShapeDtypeStruct((rows_dev, cut), F32)
    stay, share = pl.pallas_call(
        blend_kernel,
        name="blend",
        compiler_params=SMALL,
        out_shape=(factors, factors),
        in_specs=[smem, vmem, vmem],
        out_specs=(vmem, vmem),
    )(roughness, class_map, beside)

    *items, stay, share = lax.optimization_barrier((*items, stay, share))
    keep, give = stamp(items, hops, rows_dev, cols_dev, map_cols)
    got = lax.ppermute(give, "tile", swap)
    return pl.pallas_call(
        smooth_kernel,
        name="smooth",
        compiler_params=SMALL,
        out_shape=jax.ShapeDtypeStruct((rows_dev, cols_dev), F32),
        in_specs=[smem, vmem, vmem, vmem, vmem],
        out_specs=pl.BlockSpec(memory_space=pl.ANY),
        scratch_shapes=[
            pltpu.VMEM((2, 2, HALO, cut), F32),
            pltpu.VMEM((window + 2 * HALO, cut), F32),
            pltpu.VMEM((window + 2 * HALO, cut), F32),
            pltpu.VMEM((rows_dev, cols_dev), F32),
            pltpu.SemaphoreType.DMA((2,)),
        ],
    )(roughness, keep, got, stay, share)


def solution(mesh):
    return jax.shard_map(
        window_map,
        mesh=mesh,
        in_specs=(
            P(("grp", "storm", "tile"), None, None, None),
            P(("grp", "storm", "tile"), None),
            P(("grp", "storm", "tile")),
            P(("grp", "storm", "tile")),
            P(("grp", "storm", "tile")),
            P(("grp", "storm"), "tile"),
            P(),
        ),
        out_specs=P(("grp", "storm"), "tile"),
        check_vma=False,
    )
```
